32 devices in a mesh: wide: 8 (over y, x, core), quad: 4 (over z).
Axes of the slice: x: 2, y: 2, z: 4, core: 2. Of those that a mesh axis runs over, the one named last changes fastest.
Arguments:
- basis: float32 [16, 2097152], P(None, ('wide', 'quad')), may hold values from -6 to 6
- target: float32 [2097152], P(('wide', 'quad')), may hold values from -6 to 6
- sign_bits: int32 [2097152], P(('wide', 'quad')), may hold values from 0 to 1
- samples: int32 [8192], replicated, may hold values from 0 to 2097151
- owners: int32 [8192], replicated, may hold values from 0 to 7
Outputs:
- sketch: float32 [8192, 17], P(('wide', 'quad'))
- gram: float32 [8, 16, 17], P('quad')
The draws below stay inside these ranges and needn't reach their ends.
Inputs may be any that keep to these rules, and one draw needn't show every extreme that they name: `samples`: sampled scenarios may repeat.
All inputs are finite; a program needn't handle non-finite values.
Results may differ from the reference program's by a relative error of at most 0.0003.
Values sent between devices are 32-bit elements; how exact they have to be, the bound alone decides.
A program may use at most 128 MiB of HBM per device.

```python
import math
import jax
import jax.numpy as jnp
import numpy as np
from jax import lax

COLS = 16
ROWS_DEV = 65536
SCEN = 2097152
SAMPLES = 8192
GROUPS = 8
N_WIDE = 8
N_QUAD = 4


def plant(entries, rng, smallest, largest):
    shape = entries.shape
    index_at = [jax.random.randint(jax.random.fold_in(rng, axis), (), 0, shape[axis]) for axis in range(len(shape))]
    entries = entries.at[tuple(index_at)].set(smallest)
    longest = shape.index(max(shape))
    index_at[longest] = (index_at[longest] + 1) % shape[longest]
    return entries.at[tuple(index_at)].set(largest)


def level_of(own_key, shape, cuts, least, high):
    loudness = 1.0
    for axis_at, shards_of in cuts:
        draws = jax.random.uniform(jax.random.fold_in(jax.random.fold_in(own_key, 6), axis_at), (shards_of,), jnp.float32, least / len(cuts), high / len(cuts))
        loudness = loudness * jnp.repeat(jnp.exp(draws), shape[axis_at] // shards_of).reshape((-1,) + (1,) * (len(shape) - 1 - axis_at))
    return loudness


def rank_table(number_of, lean):
    portions = [(1 << 20) // math.isqrt(standing ** lean) + 1 for standing in range(1, number_of + 1)]
    deviation = 1 + sum(portions) // (1 << 30)
    return np.cumsum(np.array([max(1, weight // deviation) for weight in portions]))


def ranked(rng, shape, count, slope):
    table = rank_table(count, slope)
    pick = jax.random.randint(jax.random.fold_in(rng, 1), shape, 0, int(table[count - 1]))
    rank = jnp.searchsorted(jnp.asarray(table, jnp.int32), pick, side="right")
    return jax.random.permutation(jax.random.fold_in(rng, 2), count)[rank].astype(jnp.int32)


def bell_draw(key, shape, scale, reach, cuts=(), kind=jnp.bfloat16):
    drawn = scale * jax.random.normal(key, shape, jnp.float32)
    if cuts:
        drawn = drawn * level_of(key, shape, cuts, -0.22, 0.18)
    return jnp.clip(drawn, -reach, reach).astype(kind)


def setup_inputs(seed: int = 0) -> dict:
    seeds = jax.random.split(jax.random.key(seed), 6)
    return {
        "basis": bell_draw(seeds[0], (COLS, SCEN), 1.0, 6.0, ((1, 32),), jnp.float32),
        "target": bell_draw(seeds[1], (SCEN,), 1.0, 6.0, ((0, 32),), jnp.float32),
        "sign_bits": plant(jax.random.randint(seeds[2], (SCEN,), 0, 2), jax.random.fold_in(seeds[2], 1), 0, 1).astype(jnp.int32),
        "samples": plant(jax.random.randint(seeds[3], (SAMPLES,), 0, SCEN), jax.random.fold_in(seeds[3], 1), 0, SCEN - 1).astype(jnp.int32),
        "owners": plant(ranked(seeds[4], (SAMPLES,), GROUPS, 2), jax.random.fold_in(seeds[4], 3), 0, GROUPS - 1).astype(jnp.int32),
    }


def butterfly(field):
    width, length = field.shape
    half = 1
    while half < length:
        split = field.reshape(width, length // (2 * half), 2, half)
        upper = split[:, :, 0, :]
        lower = split[:, :, 1, :]
        field = jnp.stack([upper + lower, upper - lower], axis=2).reshape(width, length)
        half = half * 2
    return field


def parity_sign(first, second, nbits):
    count = jnp.zeros_like(first)
    for bit in range(nbits):
        count = count + ((first & second) >> bit) & 1
    return (1 - 2 * (count & 1)).astype(jnp.float32)


def reference(basis, target, sign_bits, samples, owners):
    devices = N_WIDE * N_QUAD
    rows = ROWS_DEV
    nbits = devices.bit_length() - 1
    dev_of = (samples // rows).astype(jnp.int32)
    pos_of = (samples % rows).astype(jnp.int32)
    scale = 1.0 / float(SCEN) ** 0.5

    def step(carry, dev):
        start = (dev * rows).astype(jnp.int32)
        part_basis = lax.dynamic_slice_in_dim(basis, start, rows, 1)
        part_target = lax.dynamic_slice_in_dim(target, start, rows, 0)
        part_bits = lax.dynamic_slice_in_dim(sign_bits, start, rows, 0)
        flip = (1 - 2 * part_bits).astype(jnp.float32)
        signed = jnp.concatenate([part_basis, part_target[None, :]], axis=0) * flip[None, :]
        local = butterfly(signed)
        values = jnp.take(local, pos_of, axis=1)
        sign = parity_sign(dev_of, jnp.full_like(dev_of, dev), nbits)
        return carry + values * sign[None, :], None

    init = jnp.zeros((COLS + 1, SAMPLES), jnp.float32)
    total, _ = lax.scan(step, init, jnp.arange(devices, dtype=jnp.int32))
    sketch = (total * scale).T
    onehot = (owners[:, None] == jnp.arange(GROUPS, dtype=jnp.int32)[None, :]).astype(jnp.float32)
    gram = jnp.einsum("rg,ri,rj->gij", onehot, sketch[:, :COLS], sketch, precision=lax.Precision.HIGHEST)
    gram = gram * (GROUPS / SAMPLES)
    return sketch, gram
```

```python
import functools
import math

import jax
import jax.numpy as jnp
from jax import lax
from jax.experimental import pallas as pl
from jax.experimental.pallas import tpu as pltpu
from jax.sharding import PartitionSpec as P

GROUPS = 8
LANES = 128
LINE = 256
HIGH = 8
SLOT = 32
MESH = pl.DeviceIdType.MESH


def bits_of(n):
    return n.bit_length() - 1


def parity(x, nbits):
    shift = 1
    while shift < nbits:
        x = x ^ (x >> shift)
        shift *= 2
    return x & 1


def butterfly(parts):
    half = 1
    while half < len(parts):
        for at in range(0, len(parts), 2 * half):
            for i in range(at, at + half):
                parts[i], parts[i + half] = parts[i] + parts[i + half], parts[i] - parts[i + half]
        half *= 2
    return parts


def place_of(high):
    return ((high & 1) * (HIGH // 2) + (high >> 1)) * SLOT


def split(x):
    top = x.astype(jnp.bfloat16)
    return top, (x - top.astype(jnp.float32)).astype(jnp.bfloat16)


def contract_last(a, b, **kw):
    return lax.dot_general(a, b, (((1,), (1,)), ((), ())), preferred_element_type=jnp.float32, **kw)


def sketch_kernel(
    n_wide, n_quad, scale, samp_in, owners_in, bits_in, x_in, t_in, sketch, gram,
    bits_all, x_all, t_all, load_sems,
    field, table, walsh, unit, samp, owners, picks, slots_all, rows_a, rows_b, sems,
    main, last, got_main, got_last, sum_main, sum_last, wide_main, wide_last,
    row_main, row_last, quad_main, quad_last, wide_gram, own_gram, quad_gram,
    mate_sends, mate_recvs, chip_sends, chip_recvs, sends, recvs
):
    chunk = x_all.shape[2]
    lines_in = chunk // LANES
    mids = chunk // LINE
    local_bits = bits_of(HIGH * chunk)
    devices, cols, per_dev = main.shape
    lines = per_dev // LANES
    wide = lax.axis_index("wide")
    quad = lax.axis_index("quad")
    me = wide * n_quad + quad
    core, chip, chips = wide % 2, wide // 2, n_wide // 2
    mate = (wide + 1 - 2 * core, quad)
    wide_peers = [((wide + k) % n_wide, quad) for k in range(1, n_wide)]
    quad_peers = [(wide, (quad + k) % n_quad) for k in range(1, n_quad)]
    barrier = pltpu.get_barrier_semaphore()

    def loads(h):
        at = pl.multiple_of(h * chunk, chunk)
        rows = pl.ds(pl.multiple_of(h * lines_in, lines_in), lines_in)
        return (
            pltpu.make_async_copy(bits_in.at[rows], bits_all.at[h], load_sems.at[0, h]),
            pltpu.make_async_copy(t_in.at[rows], t_all.at[h], load_sems.at[1, h]),
            pltpu.make_async_copy(x_in.at[:, pl.ds(at, chunk)], x_all.at[h], load_sems.at[2, h]),
        )

    samp_copy = pltpu.make_async_copy(samp_in, samp, sems.at[0])
    owners_copy = pltpu.make_async_copy(owners_in, owners, sems.at[1])
    samp_copy.start()
    for h in range(HIGH):
        for copy in loads(h):
            copy.start()
    owners_copy.start()
    for peer in wide_peers + quad_peers:
        pl.semaphore_signal(barrier, inc=1, device_id=peer, device_id_type=MESH)
    a = lax.broadcasted_iota(jnp.int32, (LINE, LINE), 0)
    b = lax.broadcasted_iota(jnp.int32, (LINE, LINE), 1)
    line = (1 - 2 * parity(a & b, bits_of(LINE))).astype(jnp.float32).astype(jnp.bfloat16)
    walsh[:, :LINE] = line
    walsh[:, LINE:] = line
    a = lax.broadcasted_iota(jnp.int32, (LANES, LANES), 0)
    b = lax.broadcasted_iota(jnp.int32, (LANES, LANES), 1)
    line = jnp.where(a == b, 1.0, 0.0).astype(jnp.bfloat16)
    unit[:, :LANES] = line
    unit[:, LANES:] = line
    samp_copy.wait()
    picks[...] = samp[...] & (table.shape[0] - 1)
    picks_copy = pltpu.make_async_copy(picks, slots_all, sems.at[2])
    picks_copy.start()

    row = lax.broadcasted_iota(jnp.int32, (8, LANES), 0)

    def first_pass(high, carry):
        for copy in loads(high):
            copy.wait()
        bits, t, x = bits_all.at[high], t_all.at[high], x_all.at[high]
        base = pl.multiple_of(place_of(high), SLOT)
        for part in range(LINE // LANES):
            for tile in range(cols // 8 + 1):
                values = []
                for mid in range(mids):
                    line = mid * (LINE // LANES) + part
                    flip = (1 - 2 * bits[line : line + 1, :]).astype(jnp.float32)
                    if tile < cols // 8:
                        value = x[tile * 8 : tile * 8 + 8, line * LANES : (line + 1) * LANES] * flip
                    else:
                        value = jnp.where(row == 0, t[line : line + 1, :] * flip, 0.0)
                    values.append(value)
                for mid, value in enumerate(butterfly(values)):
                    field[mid, pl.ds(base + tile * 8, 8), part * LANES : (part + 1) * LANES] = value
        return carry

    lax.fori_loop(0, HIGH, first_pass, 0)
    used = cols + 8

    def mix(mid, carry):
        halves = []
        for part in range(LINE // LANES):
            values = [
                field[mid, place_of(h) : place_of(h) + used, part * LANES : (part + 1) * LANES]
                for h in range(HIGH)
            ]
            values = butterfly(values)
            order = sorted(range(HIGH), key=place_of)
            blank = jnp.zeros((SLOT - used, LANES), jnp.float32)
            halves.append(jnp.concatenate([p for h in order for p in (values[h], blank)], axis=0))
        both = jnp.concatenate(split(jnp.concatenate(halves, axis=1)), axis=1)
        out = contract_last(walsh[...], both)
        at = pl.multiple_of(mid * LINE, LINE)
        table[pl.ds(at, LINE), :] = out[:, :LANES]
        table[pl.ds(at + mids * LINE, LINE), :] = out[:, LANES:]
        return carry

    lax.fori_loop(0, mids, mix, 0, unroll=8)
    table_rows = table.shape[0]
    half = devices // 2

    def chip_at(k):
        return (chip + 1 + k) % chips

    def device_at(slot):
        to_core = (core + 1 + slot // half) % 2
        to_wide = chip_at(slot // n_quad % chips) * 2 + to_core
        return to_wide * n_quad + slot % n_quad

    def gather(slot, rows):
        dev = device_at(jnp.minimum(slot, devices - 1))
        for r in range(per_dev):
            rows[r : r + 1, :] = table[pl.ds(slots_all[dev, r // LANES, r % LANES], 1), :]

    def finish(slot, rows):
        dev = device_at(slot)
        out = contract_last(unit[...], jnp.concatenate(split(rows[...]), axis=1))
        number = jnp.concatenate([samp[dev, i : i + 1] for i in range(lines)], axis=1)
        group = (number >> bits_of(table_rows)) & (LANES // SLOT - 1)
        sign = parity((number >> local_bits) & me, bits_of(devices))
        sign = (1 - 2 * sign).astype(jnp.float32) * scale
        total = jnp.zeros((used, per_dev), jnp.float32)
        for g in range(LANES // SLOT):
            total = jnp.where(group == g, out[g * SLOT : g * SLOT + used, :], total)
        total = total * sign
        main[slot] = total[:cols]
        for i in range(lines):
            last[pl.ds(slot * lines + i, 1), :] = total[cols : cols + 1, i * LANES : (i + 1) * LANES]

    def remote(src, dst, send_sem, recv_sem, peer):
        return pltpu.make_async_remote_copy(
            src_ref=src, dst_ref=dst, send_sem=send_sem, recv_sem=recv_sem,
            device_id=peer, device_id_type=MESH,
        )

    tall = n_quad * lines

    def group_of(k):
        return pl.ds(k * n_quad, n_quad), pl.ds(pl.multiple_of(k * tall, 8), tall)

    def mate_copies(k):
        at, at_last = group_of(k)
        return (
            remote(main.at[at], got_main.at[at], mate_sends.at[k], mate_recvs.at[k], mate),
            remote(
                last.at[at_last], got_last.at[at_last],
                mate_sends.at[chips + k], mate_recvs.at[chips + k], mate,
            ),
        )

    def chip_copies(k):
        at, at_last = group_of(k)
        peer = (chip_at(k) * 2 + core, quad)
        return (
            remote(sum_main.at[at], wide_main.at[k], chip_sends.at[k], chip_recvs.at[k], peer),
            remote(
                sum_last.at[at_last], wide_last.at[k],
                chip_sends.at[chips + k], chip_recvs.at[chips + k], peer,
            ),
        )

    picks_copy.wait()
    owners_copy.wait()
    gather(0, rows_a)
    pl.semaphore_wait(barrier, len(wide_peers) + len(quad_peers))

    def pair(i, carry):
        slot = 2 * i
        gather(slot + 1, rows_b)
        finish(slot, rows_a)
        gather(slot + 2, rows_a)
        finish(slot + 1, rows_b)
        return carry

    def step(k, carry):
        lax.fori_loop(k * n_quad // 2, (k + 1) * n_quad // 2, pair, 0)

        @pl.when(k < chips)
        def _():
            for copy in mate_copies(k):
                copy.start()

        @pl.when(k >= chips)
        def _():
            own = k - chips
            for copy in mate_copies(own):
                copy.wait_recv()
            at, at_last = group_of(own)
            from_at, from_last = group_of(k)
            sum_main[at] = main[from_at] + got_main[at]
            sum_last[at_last, :] = last[from_last, :] + got_last[at_last, :]

            @pl.when(own < chips - 1)
            def _():
                for copy in chip_copies(own):
                    copy.start()

        return carry

    lax.fori_loop(0, 2 * chips, step, 0)
    for k in range(chips):
        for copy in mate_copies(k):
            copy.wait_send()
    for k in range(chips - 1):
        for copy in chip_copies(k):
            copy.wait()

    def add_row(to):
        row = sum_main[(chips - 1) * n_quad + to]
        for k in range(chips - 1):
            row = row + wide_main[k, to]
        row_main[to] = row

    sem_at = [0]

    def send(src, dst, peer):
        sem = sem_at[0]
        sem_at[0] += 1
        copy = remote(src, dst, sends.at[sem], recvs.at[sem], peer)
        copy.start()
        return copy

    ends = sum_last[(chips - 1) * tall :, :]
    for k in range(chips - 1):
        ends = ends + wide_last[k]
    row_last[...] = ends
    copies = []
    for k, peer in enumerate(quad_peers):
        add_row(peer[1])
        copies.append(send(row_main.at[peer[1]], quad_main.at[k], peer))
        copies.append(send(row_last, quad_last.at[k], peer))
    add_row(quad)
    for copy in copies:
        copy.wait()
    total = row_main[quad]
    ends = [row_last[pl.ds(quad * lines + i, 1), :] for i in range(lines)]
    for k in range(n_quad - 1):
        total = total + quad_main[k]
        ends = [e + quad_last[k, pl.ds(quad * lines + i, 1), :] for i, e in enumerate(ends)]
    end = jnp.concatenate(ends, axis=1)
    sketch[:cols, :] = total
    sketch[cols : cols + 1, :] = end

    group = jnp.concatenate([owners[me, i : i + 1] for i in range(lines)], axis=1)
    first = lax.broadcasted_iota(jnp.int32, (8, per_dev), 0) == 0
    right = jnp.concatenate([total, jnp.where(first, end, 0.0)], axis=0)
    left = jnp.concatenate([jnp.where(group == g, total, 0.0) for g in range(GROUPS)], axis=0)
    part = contract_last(right, left, precision=lax.Precision.HIGHEST)
    part = part * (GROUPS / (per_dev * devices))
    span = GROUPS * cols // n_quad
    block = lax.broadcasted_iota(jnp.int32, (8, LANES), 1) // span
    for q in range(n_quad):
        packed = jnp.zeros((8, LANES), jnp.float32)
        for tile in range(part.shape[0] // 8):
            turned = part[tile * 8 : tile * 8 + 8, :]
            if (tile - q) % n_quad:
                turned = pltpu.roll(turned, (tile - q) % n_quad * span, 1)
            packed = jnp.where(block == tile, turned, packed)
        own_gram[q] = packed
    copies = [send(own_gram.at[peer[1]], quad_gram.at[k], peer) for k, peer in enumerate(quad_peers)]
    for copy in copies:
        copy.wait()
    packed = own_gram[quad]
    for k in range(n_quad - 1):
        packed = packed + quad_gram[k]
    wide_gram[0] = packed
    copies = [send(wide_gram.at[0], wide_gram.at[k + 1], peer) for k, peer in enumerate(wide_peers)]
    for copy in copies:
        copy.wait()
    packed = wide_gram[wide]
    for w in range(1, n_wide):
        packed = packed + wide_gram[(wide + n_wide - w) % n_wide]
    gram[...] = packed


def finish_kernel(sketch_in, gram_in, sketch, gram):
    owned, cols, width = gram.shape
    sketch[...] = sketch_in[...]
    turned = gram_in[...].T
    for tile in range(-(-width // 8)):
        columns = min(8, width - tile * 8)
        for g in range(owned):
            at = (tile * owned + g) * cols
            gram[g, :, tile * 8 : tile * 8 + columns] = turned[at : at + cols, :columns]


def shards(n_wide, n_quad, basis, target, sign_bits, samples, owners):
    cols, rows = basis.shape
    devices = n_wide * n_quad
    total_samples = samples.shape[0]
    per_dev = total_samples // devices
    lines = per_dev // LANES
    scale = 1.0 / math.sqrt(rows * devices)
    chunk = rows // HIGH
    mids = chunk // LINE
    vmem = pl.BlockSpec(memory_space=pltpu.VMEM)
    f32 = jnp.float32
    half, chips = devices // 2, n_wide // 2
    flat = (8, LANES)
    spaces = [
        (devices, cols, per_dev), (devices * lines, LANES),
        (half, cols, per_dev), (half * lines, LANES),
        (half, cols, per_dev), (half * lines, LANES),
        (chips - 1, n_quad, cols, per_dev), (chips - 1, n_quad * lines, LANES),
        (n_quad, cols, per_dev), (n_quad * lines, LANES),
        (n_quad - 1, cols, per_dev), (n_quad - 1, n_quad * lines, LANES),
        (n_wide, *flat), (n_quad, *flat), (n_quad - 1, *flat),
    ]
    copies = [2 * chips, 2 * chips, 3 * (n_quad - 1) + n_wide - 1]
    sketch, gram = pl.pallas_call(
        functools.partial(sketch_kernel, n_wide, n_quad, scale),
        out_shape=(
            jax.ShapeDtypeStruct((cols + 1, per_dev), f32),
            jax.ShapeDtypeStruct(flat, f32),
        ),
        in_specs=[
            pl.BlockSpec(memory_space=pl.ANY),
            pl.BlockSpec(memory_space=pl.ANY),
            pl.BlockSpec(memory_space=pl.ANY),
            pl.BlockSpec(memory_space=pl.ANY),
            pl.BlockSpec(memory_space=pl.ANY),
        ],
        out_specs=(vmem, vmem),
        scratch_shapes=[
            pltpu.VMEM((HIGH, chunk // LANES, LANES), jnp.int32),
            pltpu.VMEM((HIGH, cols, chunk), f32),
            pltpu.VMEM((HIGH, chunk // LANES, LANES), f32),
            pltpu.SemaphoreType.DMA((3, HIGH)),
            pltpu.VMEM((mids, HIGH * SLOT, LINE), f32),
            pltpu.VMEM((rows * SLOT // LANES, LANES), f32),
            pltpu.VMEM((LINE, 2 * LINE), jnp.bfloat16),
            pltpu.VMEM((LANES, 2 * LANES), jnp.bfloat16),
            pltpu.VMEM((devices, lines, LANES), jnp.int32),
            pltpu.VMEM((devices, lines, LANES), jnp.int32),
            pltpu.VMEM((devices, lines, LANES), jnp.int32),
            pltpu.SMEM((devices, lines, LANES), jnp.int32),
            pltpu.VMEM((per_dev, LANES), f32),
            pltpu.VMEM((per_dev, LANES), f32),
            pltpu.SemaphoreType.DMA((3,)),
        ]
        + [pltpu.VMEM(space, f32) for space in spaces]
        + [pltpu.SemaphoreType.DMA((n,)) for n in copies for _ in range(2)],
        compiler_params=pltpu.CompilerParams(
            vmem_limit_bytes=60 * 1024 * 1024, collective_id=0, has_side_effects=True
        ),
    )(
        samples.reshape(devices, lines, LANES),
        owners.reshape(devices, lines, LANES),
        sign_bits.reshape(-1, LANES),
        basis,
        target.reshape(-1, LANES),
    )
    sketch, gram = pl.pallas_call(
        finish_kernel,
        out_shape=(
            jax.ShapeDtypeStruct((cols + 1, per_dev), f32),
            jax.ShapeDtypeStruct((GROUPS // n_quad, cols, cols + 1), f32),
        ),
        in_specs=[vmem, vmem],
        out_specs=(vmem, vmem),
    )(sketch, gram)
    return sketch.T, gram


def solution(mesh):
    placed = (P(None, ("wide", "quad")), P(("wide", "quad")), P(("wide", "quad")), P(), P())
    return jax.shard_map(
        functools.partial(shards, mesh.shape["wide"], mesh.shape["quad"]),
        mesh=mesh,
        in_specs=placed,
        out_specs=(P(("wide", "quad"), None), P("quad", None, None)),
        check_vma=False,
    )
```

```python
import functools
import math

import jax
import jax.numpy as jnp
from jax import lax
from jax.experimental import pallas as pl
from jax.experimental.pallas import tpu as pltpu
from jax.sharding import PartitionSpec as P

GROUPS = 8
LANES = 128
LINE = 256
HIGH = 8
MESH = pl.DeviceIdType.MESH


def bits_of(n):
    return n.bit_length() - 1


def parity(x, nbits):
    shift = 1
    while shift < nbits:
        x = x ^ (x >> shift)
        shift *= 2
    return x & 1


def butterfly(parts):
    half = 1
    while half < len(parts):
        for at in range(0, len(parts), 2 * half):
            for i in range(at, at + half):
                parts[i], parts[i + half] = parts[i] + parts[i + half], parts[i] - parts[i + half]
        half *= 2
    return parts


def split(x):
    top = x.astype(jnp.bfloat16)
    return top, (x - top.astype(jnp.float32)).astype(jnp.bfloat16)


def contract_last(a, b, **kw):
    return lax.dot_general(a, b, (((1,), (1,)), ((), ())), preferred_element_type=jnp.float32, **kw)


def sketch_kernel(
    n_wide, n_quad, scale, samp_in, owners_in, bits_in, x_in, t_in, sketch, gram,
    bits_all, x_all, t_all, load_sems, flips,
    field, spare, table, walsh, unit, samp, owners, picks, slot_of, sign_of, slots, rows_of, sems, pick_sems,
    mine, got, sums, wide_in, row, quad_in, wide_gram, own_gram, quad_gram,
    mate_sends, mate_recvs, chip_sends, chip_recvs, sends, recvs
):
    chunk = x_all.shape[2]
    lines_in = chunk // LANES
    parts = LINE // LANES
    mids = chunk // LINE
    local_bits = bits_of(HIGH * chunk)
    cols = x_all.shape[1]
    devices = n_wide * n_quad
    lines = samp.shape[0] // devices
    per_dev = lines * LANES
    kept = LANES // (cols + 1)
    ends_at = kept * cols
    spill_blocks = -(-mids // kept)
    wide = lax.axis_index("wide")
    quad = lax.axis_index("quad")
    me = wide * n_quad + quad
    core, chip, chips = wide % 2, wide // 2, n_wide // 2
    mate = (wide + 1 - 2 * core, quad)
    wide_peers = [((wide + k) % n_wide, quad) for k in range(1, n_wide)]
    quad_peers = [(wide, (quad + k) % n_quad) for k in range(1, n_quad)]
    barrier = pltpu.get_barrier_semaphore()

    def loads(h):
        at = pl.multiple_of(h * chunk, chunk)
        rows = pl.ds(pl.multiple_of(h * lines_in, lines_in), lines_in)
        return (
            pltpu.make_async_copy(bits_in.at[rows], bits_all.at[rows], load_sems.at[0, h]),
            pltpu.make_async_copy(t_in.at[rows], t_all.at[rows], load_sems.at[1, h]),
            pltpu.make_async_copy(x_in.at[:, pl.ds(at, chunk)], x_all.at[h], load_sems.at[2, h]),
        )

    samp_copy = pltpu.make_async_copy(samp_in, samp, sems.at[0])
    owners_copy = pltpu.make_async_copy(owners_in, owners, sems.at[1])
    samp_copy.start()
    for h in range(HIGH):
        for copy in loads(h):
            copy.start()
    owners_copy.start()
    for peer in wide_peers + quad_peers:
        pl.semaphore_signal(barrier, inc=1, device_id=peer, device_id_type=MESH)
    a = lax.broadcasted_iota(jnp.int32, (LINE, LINE), 0)
    b = lax.broadcasted_iota(jnp.int32, (LINE, LINE), 1)
    line = (1 - 2 * parity(a & b, bits_of(LINE))).astype(jnp.float32).astype(jnp.bfloat16)
    walsh[:, :LINE] = line
    walsh[:, LINE:] = line
    a = lax.broadcasted_iota(jnp.int32, (LANES, LANES), 0)
    b = lax.broadcasted_iota(jnp.int32, (LANES, LANES), 1)
    line = jnp.where(a == b, 1.0, 0.0).astype(jnp.bfloat16)
    unit[:, :LANES] = line
    unit[:, LANES:] = line
    pad = t_all.shape[0] - HIGH * lines_in
    t_all[HIGH * lines_in :, :] = jnp.zeros((pad, LANES), jnp.float32)

    samp_copy.wait()
    number = samp[...]
    mid_of = (number >> bits_of(LINE)) & (mids - 1)
    high_of = (number >> bits_of(chunk)) & (HIGH - 1)
    block = jnp.zeros_like(mid_of)
    for i in range(1, spill_blocks):
        block = block + jnp.where(mid_of >= i * kept, 1, 0)
    spilled = high_of >= kept
    picks[...] = jnp.where(spilled, mids + block, mid_of) * LINE + (number & (LINE - 1))
    slot_of[...] = jnp.where(spilled, mid_of - kept * block, high_of)
    sign = parity((number >> local_bits) & me, bits_of(devices))
    sign_of[...] = (1 - 2 * sign).astype(jnp.float32) * scale

    def chip_at(k):
        return (chip + 1 + k) & (chips - 1)

    def base_of(group, own):
        to_core = (core + 1 + own) & 1
        return (chip_at(group) * 2 + to_core) * n_quad

    def even_base(turn):
        group = jnp.minimum(jnp.maximum(turn - 1, 0), chips - 1)
        return base_of(group, jnp.minimum(turn, 1))

    def odd_base(turn):
        return base_of(jnp.minimum(turn + 1, chips - 1), (turn + 1) >> bits_of(chips))

    def fetch(dev, buf):
        at = pl.ds(dev * lines, lines)
        return pltpu.make_async_copy(picks.at[at], slots.at[buf], pick_sems.at[buf])

    def fetch_even(turn):
        base, after = even_base(turn), odd_base(turn)
        return [fetch(base + j if j < n_quad else after, j - 1) for j in range(1, n_quad + 1)]

    def fetch_odd(turn):
        base, after = odd_base(turn), even_base(turn + 1)
        return [fetch(base + j if j < n_quad else after, n_quad + j - 1) for j in range(1, n_quad + 1)]

    first_fetch = fetch(even_base(0), 2 * n_quad)
    for copy in [first_fetch] + fetch_even(0) + fetch_odd(0):
        copy.start()

    low = lax.broadcasted_iota(jnp.int32, (8, LANES), 0)
    signs = [1.0 - 2.0 * ((low >> i) & 1).astype(jnp.float32) for i in range(3)]

    def across(x, i):
        step = 1 << i
        down = pltpu.roll(x, step, 0)
        if step == 4:
            return x * signs[i] + down
        return x * signs[i] + jnp.where(signs[i] < 0, down, pltpu.roll(x, 8 - step, 0))

    def first_pass(high, carry):
        for copy in loads(high):
            copy.wait()
        rows = pl.ds(pl.multiple_of(high * lines_in, lines_in), lines_in)
        flip = (1 - 2 * bits_all[rows]).astype(jnp.float32)
        flips[...] = flip
        t = t_all[rows] * flip
        t = butterfly([t[i * 8 : i * 8 + 8] for i in range(lines_in // 8)])
        for i in range(bits_of(parts), 3):
            t = [across(x, i) for x in t]
        for i, value in enumerate(t):
            t_all[pl.ds(pl.multiple_of(high * lines_in + i * 8, 8), 8), :] = value
        x = x_all.at[high]
        at = pl.multiple_of(high * cols, cols)
        for part in range(parts):
            for tile in range(cols // 8):
                values = []
                for mid in range(mids):
                    line = mid * parts + part
                    flip = flips[pl.ds(line, 8, stride=0), :]
                    values.append(x[tile * 8 : tile * 8 + 8, line * LANES : (line + 1) * LANES] * flip)
                for mid, value in enumerate(butterfly(values)):
                    field[mid, pl.ds(at + tile * 8, 8), part * LANES : (part + 1) * LANES] = value
        return carry

    lax.fori_loop(0, HIGH, first_pass, 0)
    for i in range(lines_in // 8):
        t = butterfly([t_all[h * lines_in + i * 8 : h * lines_in + i * 8 + 8, :] for h in range(HIGH)])
        for h, value in enumerate(t):
            t_all[h * lines_in + i * 8 : h * lines_in + i * 8 + 8, :] = value
    blank = jnp.zeros((LANES - ends_at - 8, LANES), jnp.float32)

    def change(blocks, at):
        both = jnp.concatenate(split(jnp.concatenate(blocks, axis=0)), axis=1)
        out = contract_last(walsh[...], both)
        for i in range(len(blocks)):
            table[pl.ds(at + i * LINE, LINE), :] = out[:, i * LANES : (i + 1) * LANES]

    def mix(pair, carry):
        blocks = []
        for i in range(2):
            mid = 2 * pair + i
            halves = []
            for part in range(parts):
                across_lanes = slice(part * LANES, (part + 1) * LANES)
                values = [
                    butterfly([field[mid, h * cols + r : h * cols + r + 8, across_lanes] for h in range(HIGH)])
                    for r in range(0, cols, 8)
                ]
                for r, value in enumerate(values):
                    spare[mid, r * 8 : r * 8 + 8, across_lanes] = value[kept]
                t = t_all[pl.ds(mid * parts + part, 8, stride=lines_in), :]
                mains = [value[h] for h in range(kept) for value in values]
                halves.append(jnp.concatenate(mains + [t, blank], axis=0))
            blocks.append(jnp.concatenate(halves, axis=1))
        change(blocks, pl.multiple_of(pair * 2 * LINE, 2 * LINE))
        return carry

    lax.fori_loop(0, mids // 2, mix, 0, unroll=4)
    for first in range(0, spill_blocks, 2):
        blocks = []
        for i in range(first, min(first + 2, spill_blocks)):
            halves = []
            for part in range(parts):
                across_lanes = slice(part * LANES, (part + 1) * LANES)
                mains = [
                    spare[mid, :, across_lanes] if mid < mids else jnp.zeros((cols, LANES), jnp.float32)
                    for mid in range(i * kept, (i + 1) * kept)
                ]
                t = t_all[pl.ds(kept * lines_in + i * kept * parts + part, 8, stride=parts), :]
                halves.append(jnp.concatenate(mains + [t, blank], axis=0))
            blocks.append(jnp.concatenate(halves, axis=1))
        change(blocks, (mids + first) * LINE)

    def gather(buf, at):
        for r in range(per_dev):
            rows_of[at, r : r + 1, :] = table[pl.ds(slots[buf, r // LANES, r % LANES], 1), :]

    def finish(slot, dev, at):
        out = contract_last(unit[...], jnp.concatenate(split(rows_of[at]), axis=1))
        for i in range(lines):
            group = slot_of[pl.ds(dev * lines + i, 8, stride=0), :]
            sign = sign_of[pl.ds(dev * lines + i, 8, stride=0), :]
            half = out[:, i * LANES : (i + 1) * LANES]
            for r in range(0, cols, 8):
                total = half[r : r + 8]
                for g in range(1, kept):
                    total = jnp.where(group == g, half[g * cols + r : g * cols + r + 8], total)
                mine[slot, i * cols + r : i * cols + r + 8, :] = total * sign
            end = jnp.where(low == group, half[ends_at : ends_at + 8], 0.0)
            end = jnp.sum(end, axis=0, keepdims=True) * sign[:1]
            mine[slot, lines * cols + i : lines * cols + i + 1, :] = end

    def remote(src, dst, send_sem, recv_sem, peer):
        return pltpu.make_async_remote_copy(
            src_ref=src, dst_ref=dst, send_sem=send_sem, recv_sem=recv_sem,
            device_id=peer, device_id_type=MESH,
        )

    def group_of(k):
        return pl.ds(k * n_quad, n_quad)

    def mate_copy(k):
        at = group_of(k)
        return remote(mine.at[at], got.at[at], mate_sends.at[k], mate_recvs.at[k], mate)

    def chip_copy(k):
        peer = (chip_at(k) * 2 + core, quad)
        return remote(sums.at[group_of(k)], wide_in.at[k], chip_sends.at[k], chip_recvs.at[k], peer)

    def own_sum(group):
        mate_copy(group).wait_recv()
        at = group_of(group)
        sums[at] = mine[group_of(chips + group)] + got[at]

    first_fetch.wait()
    gather(2 * n_quad, 0)
    pl.semaphore_wait(barrier, len(wide_peers) + len(quad_peers))
    owners_copy.wait()

    def work(base, slot, buf, count):
        for j in range(n_quad):
            if j < count:
                gather(buf + j, (j + 1) % n_quad)
            finish(slot + j, base + j, j)

    def turns(turn, carry):
        for copy in fetch_even(turn):
            copy.wait()
        own = jnp.minimum(turn, 1)
        group = jnp.maximum(turn - 1, 0)
        work(even_base(turn), (own * chips + group) * n_quad, 0, n_quad)

        @pl.when(turn == 0)
        def _():
            mate_copy(0).start()

        @pl.when(turn > 0)
        def _():
            own_sum(turn - 1)
            chip_copy(turn - 1).start()

        @pl.when(turn < chips - 1)
        def _():
            for copy in fetch_even(turn + 1):
                copy.start()

        for copy in fetch_odd(turn):
            copy.wait()

        @pl.when(turn < chips - 1)
        def _():
            work(odd_base(turn), (turn + 1) * n_quad, n_quad, n_quad)
            mate_copy(turn + 1).start()
            for copy in fetch_odd(turn + 1):
                copy.start()

        @pl.when(turn == chips - 1)
        def _():
            work(odd_base(turn), (2 * chips - 1) * n_quad, n_quad, n_quad - 1)
            own_sum(chips - 1)

        return carry

    lax.fori_loop(0, chips, turns, 0)
    for k in range(chips):
        mate_copy(k).wait_send()
    for k in range(chips - 1):
        chip_copy(k).wait()

    def add_row(to):
        total = sums[(chips - 1) * n_quad + to]
        for k in range(chips - 1):
            total = total + wide_in[k, to]
        row[to] = total

    sem_at = [0]

    def send(src, dst, peer):
        sem = sem_at[0]
        sem_at[0] += 1
        copy = remote(src, dst, sends.at[sem], recvs.at[sem], peer)
        copy.start()
        return copy

    copies = []
    for k, peer in enumerate(quad_peers):
        add_row(peer[1])
        copies.append(send(row.at[peer[1]], quad_in.at[k], peer))
    add_row(quad)
    for copy in copies:
        copy.wait()
    total = row[quad]
    for k in range(n_quad - 1):
        total = total + quad_in[k]
    end = jnp.concatenate([total[lines * cols + i : lines * cols + i + 1] for i in range(lines)], axis=1)
    total = jnp.concatenate([total[i * cols : (i + 1) * cols] for i in range(lines)], axis=1)
    sketch[:cols, :] = total
    sketch[cols : cols + 1, :] = end

    group = jnp.concatenate([owners[pl.ds(me * lines + i, cols, stride=0), :] for i in range(lines)], axis=1)
    first = lax.broadcasted_iota(jnp.int32, (8, per_dev), 0) == 0
    right = jnp.concatenate([total, jnp.where(first, end, 0.0)], axis=0)
    left = jnp.concatenate([jnp.where(group == g, total, 0.0) for g in range(GROUPS)], axis=0)
    part = contract_last(right, left, precision=lax.Precision.HIGHEST)
    part = part * (GROUPS / (per_dev * devices))
    span = GROUPS * cols // n_quad
    block = lax.broadcasted_iota(jnp.int32, (8, LANES), 1) // span
    for q in range(n_quad):
        packed = jnp.zeros((8, LANES), jnp.float32)
        for tile in range(part.shape[0] // 8):
            turned = part[tile * 8 : tile * 8 + 8, :]
            if (tile - q) % n_quad:
                turned = pltpu.roll(turned, (tile - q) % n_quad * span, 1)
            packed = jnp.where(block == tile, turned, packed)
        own_gram[q] = packed
    copies = [send(own_gram.at[peer[1]], quad_gram.at[k], peer) for k, peer in enumerate(quad_peers)]
    for copy in copies:
        copy.wait()
    packed = own_gram[quad]
    for k in range(n_quad - 1):
        packed = packed + quad_gram[k]
    wide_gram[0] = packed
    copies = [send(wide_gram.at[0], wide_gram.at[k + 1], peer) for k, peer in enumerate(wide_peers)]
    for copy in copies:
        copy.wait()
    packed = wide_gram[wide]
    for w in range(1, n_wide):
        packed = packed + wide_gram[(wide + n_wide - w) % n_wide]
    gram[...] = packed


def finish_kernel(sketch_in, gram_in, sketch, gram):
    owned, cols, width = gram.shape
    sketch[...] = sketch_in[...]
    turned = gram_in[...].T
    for tile in range(-(-width // 8)):
        columns = min(8, width - tile * 8)
        for g in range(owned):
            at = (tile * owned + g) * cols
            gram[g, :, tile * 8 : tile * 8 + columns] = turned[at : at + cols, :columns]


def shards(n_wide, n_quad, basis, target, sign_bits, samples, owners):
    cols, rows = basis.shape
    devices = n_wide * n_quad
    total_samples = samples.shape[0]
    per_dev = total_samples // devices
    lines = per_dev // LANES
    scale = 1.0 / math.sqrt(rows * devices)
    chunk = rows // HIGH
    mids = chunk // LINE
    vmem = pl.BlockSpec(memory_space=pltpu.VMEM)
    f32 = jnp.float32
    half, chips = devices // 2, n_wide // 2
    flat = (8, LANES)
    packed = (lines * (cols + 1), LANES)
    kept = LANES // (cols + 1)
    blocks = mids + -(-mids // kept)
    spaces = [
        (devices, *packed), (half, *packed), (half, *packed), (chips - 1, n_quad, *packed),
        (n_quad, *packed), (n_quad - 1, *packed),
        (n_wide, *flat), (n_quad, *flat), (n_quad - 1, *flat),
    ]
    copies = [chips, chips - 1, 2 * (n_quad - 1) + n_wide - 1]
    sketch, gram = pl.pallas_call(
        functools.partial(sketch_kernel, n_wide, n_quad, scale),
        out_shape=(
            jax.ShapeDtypeStruct((cols + 1, per_dev), f32),
            jax.ShapeDtypeStruct(flat, f32),
        ),
        in_specs=[
            pl.BlockSpec(memory_space=pl.ANY),
            pl.BlockSpec(memory_space=pl.ANY),
            pl.BlockSpec(memory_space=pl.ANY),
            pl.BlockSpec(memory_space=pl.ANY),
            pl.BlockSpec(memory_space=pl.ANY),
        ],
        out_specs=(vmem, vmem),
        scratch_shapes=[
            pltpu.VMEM((rows // LANES, LANES), jnp.int32),
            pltpu.VMEM((HIGH, cols, chunk), f32),
            pltpu.VMEM((rows // LANES + 2 * 8, LANES), f32),
            pltpu.SemaphoreType.DMA((3, HIGH)),
            pltpu.VMEM((chunk // LANES, LANES), f32),
            pltpu.VMEM((mids, HIGH * cols, LINE), f32),
            pltpu.VMEM((mids, cols, LINE), f32),
            pltpu.VMEM((blocks * LINE, LANES), f32),
            pltpu.VMEM((LINE, 2 * LINE), jnp.bfloat16),
            pltpu.VMEM((LANES, 2 * LANES), jnp.bfloat16),
            pltpu.VMEM((devices * lines, LANES), jnp.int32),
            pltpu.VMEM((devices * lines, LANES), jnp.int32),
            pltpu.VMEM((devices * lines, LANES), jnp.int32),
            pltpu.VMEM((devices * lines, LANES), jnp.int32),
            pltpu.VMEM((devices * lines, LANES), f32),
            pltpu.SMEM((2 * n_quad + 1, lines, LANES), jnp.int32),
            pltpu.VMEM((n_quad, per_dev, LANES), f32),
            pltpu.SemaphoreType.DMA((2,)),
            pltpu.SemaphoreType.DMA((2 * n_quad + 1,)),
        ]
        + [pltpu.VMEM(space, f32) for space in spaces]
        + [pltpu.SemaphoreType.DMA((n,)) for n in copies for _ in range(2)],
        compiler_params=pltpu.CompilerParams(
            vmem_limit_bytes=60 * 1024 * 1024, collective_id=0, has_side_effects=True
        ),
    )(
        samples.reshape(-1, LANES),
        owners.reshape(-1, LANES),
        sign_bits.reshape(-1, LANES),
        basis,
        target.reshape(-1, LANES),
    )
    sketch, gram = pl.pallas_call(
        finish_kernel,
        out_shape=(
            jax.ShapeDtypeStruct((cols + 1, per_dev), f32),
            jax.ShapeDtypeStruct((GROUPS // n_quad, cols, cols + 1), f32),
        ),
        in_specs=[vmem, vmem],
        out_specs=(vmem, vmem),
    )(sketch, gram)
    return sketch.T, gram


def solution(mesh):
    placed = (P(None, ("wide", "quad")), P(("wide", "quad")), P(("wide", "quad")), P(), P())
    return jax.shard_map(
        functools.partial(shards, mesh.shape["wide"], mesh.shape["quad"]),
        mesh=mesh,
        in_specs=placed,
        out_specs=(P(("wide", "quad"), None), P("quad", None, None)),
        check_vma=False,
    )
```

```python
import functools
import math

import jax
import jax.numpy as jnp
from jax import lax
from jax.experimental import pallas as pl
from jax.experimental.pallas import tpu as pltpu
from jax.sharding import PartitionSpec as P

GROUPS = 8
LANES = 128
LINE = 256
HIGH = 8
MESH = pl.DeviceIdType.MESH


def bits_of(n):
    return n.bit_length() - 1


def parity(x, nbits):
    shift = 1
    while shift < nbits:
        x = x ^ (x >> shift)
        shift *= 2
    return x & 1


def butterfly(parts):
    half = 1
    while half < len(parts):
        for at in range(0, len(parts), 2 * half):
            for i in range(at, at + half):
                parts[i], parts[i + half] = parts[i] + parts[i + half], parts[i] - parts[i + half]
        half *= 2
    return parts


def split(x):
    top = x.astype(jnp.bfloat16)
    return top, (x - top.astype(jnp.float32)).astype(jnp.bfloat16)


def contract_last(a, b, **kw):
    return lax.dot_general(a, b, (((1,), (1,)), ((), ())), preferred_element_type=jnp.float32, **kw)


def sketch_kernel(
    n_wide, n_quad, scale, samp_in, owners_in, bits_in, x_in, t_in, sketch, gram,
    bits_all, x_all, t_all, load_sems, flips,
    field, spare, table, walsh, unit, samp, owners, picks, slot_of, sign_of, slots, rows_of, sems, pick_sems,
    mine, got, sums, wide_in, direct_in, row, quad_in, own_gram, mate_gram, pair_gram, gram_in,
    mate_sends, mate_recvs, chip_sends, chip_recvs, direct_sends, direct_recvs, sends, recvs
):
    chunk = x_all.shape[2]
    lines_in = chunk // LANES
    parts = LINE // LANES
    mids = chunk // LINE
    local_bits = bits_of(HIGH * chunk)
    cols = x_all.shape[1]
    devices = n_wide * n_quad
    lines = samp.shape[0] // devices
    per_dev = lines * LANES
    kept = LANES // (cols + 1)
    ends_at = kept * cols
    spill_blocks = -(-mids // kept)
    wide = lax.axis_index("wide")
    quad = lax.axis_index("quad")
    me = wide * n_quad + quad
    core, chip, chips = wide % 2, wide // 2, n_wide // 2
    mate = (wide + 1 - 2 * core, quad)
    peers = [
        (((chip + i) & (chips - 1)) * 2 + core, (quad + k) & (n_quad - 1))
        for i in range(chips) for k in range(n_quad)
    ]
    quad_peers = peers[1:n_quad]
    barrier = pltpu.get_barrier_semaphore()

    def loads(h):
        at = pl.multiple_of(h * chunk, chunk)
        rows = pl.ds(pl.multiple_of(h * lines_in, lines_in), lines_in)
        return (
            pltpu.make_async_copy(bits_in.at[rows], bits_all.at[rows], load_sems.at[0, h]),
            pltpu.make_async_copy(t_in.at[rows], t_all.at[rows], load_sems.at[1, h]),
            pltpu.make_async_copy(x_in.at[:, pl.ds(at, chunk)], x_all.at[h], load_sems.at[2, h]),
        )

    samp_copy = pltpu.make_async_copy(samp_in, samp, sems.at[0])
    owners_copy = pltpu.make_async_copy(owners_in, owners, sems.at[1])
    samp_copy.start()
    for h in range(HIGH):
        for copy in loads(h):
            copy.start()
    owners_copy.start()
    for peer in peers[1:] + [mate]:
        pl.semaphore_signal(barrier, inc=1, device_id=peer, device_id_type=MESH)
    a = lax.broadcasted_iota(jnp.int32, (LINE, LINE), 0)
    b = lax.broadcasted_iota(jnp.int32, (LINE, LINE), 1)
    line = (1 - 2 * parity(a & b, bits_of(LINE))).astype(jnp.float32).astype(jnp.bfloat16)
    walsh[:, :LINE] = line
    walsh[:, LINE:] = line
    a = lax.broadcasted_iota(jnp.int32, (LANES, LANES), 0)
    b = lax.broadcasted_iota(jnp.int32, (LANES, LANES), 1)
    line = jnp.where(a == b, 1.0, 0.0).astype(jnp.bfloat16)
    unit[:, :LANES] = line
    unit[:, LANES:] = line
    pad = t_all.shape[0] - HIGH * lines_in
    t_all[HIGH * lines_in :, :] = jnp.zeros((pad, LANES), jnp.float32)

    samp_copy.wait()
    number = samp[...]
    mid_of = (number >> bits_of(LINE)) & (mids - 1)
    high_of = (number >> bits_of(chunk)) & (HIGH - 1)
    block = jnp.zeros_like(mid_of)
    for i in range(1, spill_blocks):
        block = block + jnp.where(mid_of >= i * kept, 1, 0)
    spilled = high_of >= kept
    picks[...] = jnp.where(spilled, mids + block, mid_of) * LINE + (number & (LINE - 1))
    slot_of[...] = jnp.where(spilled, mid_of - kept * block, high_of)
    sign = parity((number >> local_bits) & me, bits_of(devices))
    sign_of[...] = (1 - 2 * sign).astype(jnp.float32) * scale

    def chip_at(k):
        return (chip + 1 + k) & (chips - 1)

    def base_of(group, own):
        to_core = (core + 1 + own) & 1
        return (chip_at(group) * 2 + to_core) * n_quad

    def even_of(turn):
        inner = (turn > 0) & (turn < chips - 1)
        return jnp.where(inner, turn - 1, jnp.minimum(turn, chips - 1)), jnp.where(inner, 1, 0)

    def odd_of(turn):
        own = turn >= chips - 2
        return jnp.where(own, turn, turn + 1), jnp.where(own, 1, 0)

    def even_base(turn):
        return base_of(*even_of(turn))

    def odd_base(turn):
        return base_of(*odd_of(turn))

    def fetch(dev, buf):
        at = pl.ds(dev * lines, lines)
        return pltpu.make_async_copy(picks.at[at], slots.at[buf], pick_sems.at[buf])

    def fetch_even(turn):
        base, after = even_base(turn), odd_base(turn)
        return [fetch(base + j if j < n_quad else after, j - 1) for j in range(1, n_quad + 1)]

    def fetch_odd(turn):
        base, after = odd_base(turn), even_base(turn + 1)
        return [fetch(base + j if j < n_quad else after, n_quad + j - 1) for j in range(1, n_quad + 1)]

    first_fetch = fetch(even_base(0), 2 * n_quad)
    for copy in [first_fetch] + fetch_even(0) + fetch_odd(0):
        copy.start()

    low = lax.broadcasted_iota(jnp.int32, (8, LANES), 0)
    signs = [1.0 - 2.0 * ((low >> i) & 1).astype(jnp.float32) for i in range(3)]

    def across(x, i):
        step = 1 << i
        down = pltpu.roll(x, step, 0)
        if step == 4:
            return x * signs[i] + down
        return x * signs[i] + jnp.where(signs[i] < 0, down, pltpu.roll(x, 8 - step, 0))

    def first_pass(high, carry):
        for copy in loads(high):
            copy.wait()
        rows = pl.ds(pl.multiple_of(high * lines_in, lines_in), lines_in)
        flip = (1 - 2 * bits_all[rows]).astype(jnp.float32)
        flips[...] = flip
        t = t_all[rows] * flip
        t = butterfly([t[i * 8 : i * 8 + 8] for i in range(lines_in // 8)])
        for i in range(bits_of(parts), 3):
            t = [across(x, i) for x in t]
        for i, value in enumerate(t):
            t_all[pl.ds(pl.multiple_of(high * lines_in + i * 8, 8), 8), :] = value
        x = x_all.at[high]
        at = pl.multiple_of(high * cols, cols)
        for part in range(parts):
            for tile in range(cols // 8):
                values = []
                for mid in range(mids):
                    line = mid * parts + part
                    flip = flips[pl.ds(line, 8, stride=0), :]
                    values.append(x[tile * 8 : tile * 8 + 8, line * LANES : (line + 1) * LANES] * flip)
                for mid, value in enumerate(butterfly(values)):
                    field[mid, pl.ds(at + tile * 8, 8), part * LANES : (part + 1) * LANES] = value
        return carry

    lax.fori_loop(0, HIGH, first_pass, 0)
    for i in range(lines_in // 8):
        t = butterfly([t_all[h * lines_in + i * 8 : h * lines_in + i * 8 + 8, :] for h in range(HIGH)])
        for h, value in enumerate(t):
            t_all[h * lines_in + i * 8 : h * lines_in + i * 8 + 8, :] = value
    blank = jnp.zeros((LANES - ends_at - 8, LANES), jnp.float32)

    def change(blocks, at):
        both = jnp.concatenate(split(jnp.concatenate(blocks, axis=0)), axis=1)
        out = contract_last(walsh[...], both)
        for i in range(len(blocks)):
            table[pl.ds(at + i * LINE, LINE), :] = out[:, i * LANES : (i + 1) * LANES]

    def mix(pair, carry):
        blocks = []
        for i in range(2):
            mid = 2 * pair + i
            halves = []
            for part in range(parts):
                across_lanes = slice(part * LANES, (part + 1) * LANES)
                values = [
                    butterfly([field[mid, h * cols + r : h * cols + r + 8, across_lanes] for h in range(HIGH)])
                    for r in range(0, cols, 8)
                ]
                for r, value in enumerate(values):
                    spare[mid, r * 8 : r * 8 + 8, across_lanes] = value[kept]
                t = t_all[pl.ds(mid * parts + part, 8, stride=lines_in), :]
                mains = [value[h] for h in range(kept) for value in values]
                halves.append(jnp.concatenate(mains + [t, blank], axis=0))
            blocks.append(jnp.concatenate(halves, axis=1))
        change(blocks, pl.multiple_of(pair * 2 * LINE, 2 * LINE))
        return carry

    lax.fori_loop(0, mids // 2, mix, 0, unroll=4)
    for first in range(0, spill_blocks, 2):
        blocks = []
        for i in range(first, min(first + 2, spill_blocks)):
            halves = []
            for part in range(parts):
                across_lanes = slice(part * LANES, (part + 1) * LANES)
                mains = [
                    spare[mid, :, across_lanes] if mid < mids else jnp.zeros((cols, LANES), jnp.float32)
                    for mid in range(i * kept, (i + 1) * kept)
                ]
                t = t_all[pl.ds(kept * lines_in + i * kept * parts + part, 8, stride=parts), :]
                halves.append(jnp.concatenate(mains + [t, blank], axis=0))
            blocks.append(jnp.concatenate(halves, axis=1))
        change(blocks, (mids + first) * LINE)

    def gather(buf, at):
        for r in range(per_dev):
            rows_of[at, r : r + 1, :] = table[pl.ds(slots[buf, r // LANES, r % LANES], 1), :]

    def finish(slot, dev, at):
        out = contract_last(unit[...], jnp.concatenate(split(rows_of[at]), axis=1))
        for i in range(lines):
            group = slot_of[pl.ds(dev * lines + i, 8, stride=0), :]
            sign = sign_of[pl.ds(dev * lines + i, 8, stride=0), :]
            half = out[:, i * LANES : (i + 1) * LANES]
            for r in range(0, cols, 8):
                total = half[r : r + 8]
                for g in range(1, kept):
                    total = jnp.where(group == g, half[g * cols + r : g * cols + r + 8], total)
                mine[slot, i * cols + r : i * cols + r + 8, :] = total * sign
            end = jnp.where(low == group, half[ends_at : ends_at + 8], 0.0)
            end = jnp.sum(end, axis=0, keepdims=True) * sign[:1]
            mine[slot, lines * cols + i : lines * cols + i + 1, :] = end

    def remote(src, dst, send_sem, recv_sem, peer):
        return pltpu.make_async_remote_copy(
            src_ref=src, dst_ref=dst, send_sem=send_sem, recv_sem=recv_sem,
            device_id=peer, device_id_type=MESH,
        )

    def group_of(k):
        return pl.ds(k * n_quad, n_quad)

    def mate_copy(k):
        at = group_of(k)
        return remote(mine.at[at], got.at[at], mate_sends.at[k], mate_recvs.at[k], mate)

    def chip_copy(k):
        peer = (chip_at(k) * 2 + core, quad)
        return remote(sums.at[group_of(k)], wide_in.at[k], chip_sends.at[k], chip_recvs.at[k], peer)

    def direct_copies():
        far = chips - 2
        return [
            remote(
                sums.at[far * n_quad + k], direct_in.at[quad], direct_sends.at[k], direct_recvs.at[quad],
                (chip_at(far) * 2 + core, k),
            )
            for k in range(n_quad)
        ]

    def direct_arrivals():
        return [
            remote(sums.at[0], direct_in.at[k], direct_sends.at[k], direct_recvs.at[k], peers[n_quad])
            for k in range(n_quad)
        ]

    def own_sum(group):
        mate_copy(group).wait_recv()
        at = group_of(group)
        sums[at] = mine[group_of(chips + group)] + got[at]

    first_fetch.wait()
    gather(2 * n_quad, 0)
    pl.semaphore_wait(barrier, len(peers))
    owners_copy.wait()

    def work(step, base, buf, count):
        group, own = step
        slot = (own * chips + group) * n_quad
        for j in range(n_quad):
            if j < count:
                gather(buf + j, (j + 1) % n_quad)
            finish(slot + j, base + j, j)

    def turns(turn, carry):
        for copy in fetch_even(turn):
            copy.wait()
        work(even_of(turn), even_base(turn), 0, n_quad)

        @pl.when(turn == 0)
        def _():
            mate_copy(0).start()

        @pl.when((turn > 0) & (turn < chips - 1))
        def _():
            own_sum(turn - 1)
            chip_copy(turn - 1).start()

        @pl.when(turn == chips - 1)
        def _():
            mate_copy(chips - 1).start()

        @pl.when(turn < chips - 1)
        def _():
            for copy in fetch_even(turn + 1):
                copy.start()

        for copy in fetch_odd(turn):
            copy.wait()

        @pl.when(turn < chips - 1)
        def _():
            work(odd_of(turn), odd_base(turn), n_quad, n_quad)

            @pl.when(turn < chips - 2)
            def _():
                mate_copy(turn + 1).start()

            @pl.when(turn == chips - 2)
            def _():
                own_sum(chips - 2)
                for copy in direct_copies():
                    copy.start()

            for copy in fetch_odd(turn + 1):
                copy.start()

        @pl.when(turn == chips - 1)
        def _():
            work(odd_of(turn), odd_base(turn), n_quad, n_quad - 1)
            own_sum(chips - 1)

        return carry

    lax.fori_loop(0, chips, turns, 0)
    for k in range(chips - 2):
        chip_copy(k).wait_recv()

    def add_row(to):
        total = sums[(chips - 1) * n_quad + to]
        for k in range(chips - 2):
            total = total + wide_in[k, to]
        row[to] = total

    sem_at = [0]

    def send(src, dst, peer):
        sem = sem_at[0]
        sem_at[0] += 1
        copy = remote(src, dst, sends.at[sem], recvs.at[sem], peer)
        copy.start()
        return copy

    copies = []
    for k, peer in enumerate(quad_peers):
        add_row(peer[1])
        copies.append(send(row.at[peer[1]], quad_in.at[k], peer))
    add_row(quad)
    for copy in copies:
        copy.wait()
    for copy in direct_arrivals():
        copy.wait_recv()
    total = row[quad]
    for k in range(n_quad - 1):
        total = total + quad_in[k]
    for k in range(n_quad):
        total = total + direct_in[k]
    end = jnp.concatenate([total[lines * cols + i : lines * cols + i + 1] for i in range(lines)], axis=1)
    total = jnp.concatenate([total[i * cols : (i + 1) * cols] for i in range(lines)], axis=1)
    sketch[:cols, :] = total
    sketch[cols : cols + 1, :] = end

    group = jnp.concatenate([owners[pl.ds(me * lines + i, cols, stride=0), :] for i in range(lines)], axis=1)
    first = lax.broadcasted_iota(jnp.int32, (8, per_dev), 0) == 0
    right = jnp.concatenate([total, jnp.where(first, end, 0.0)], axis=0)
    left = jnp.concatenate([jnp.where(group == g, total, 0.0) for g in range(GROUPS)], axis=0)
    part = contract_last(right, left, precision=lax.Precision.HIGHEST)
    part = part * (GROUPS / (per_dev * devices))
    span = GROUPS * cols // n_quad
    block = lax.broadcasted_iota(jnp.int32, (8, LANES), 1) // span
    for q in range(n_quad):
        packed = jnp.zeros((8, LANES), jnp.float32)
        for tile in range(part.shape[0] // 8):
            turned = part[tile * 8 : tile * 8 + 8, :]
            if (tile - q) % n_quad:
                turned = pltpu.roll(turned, (tile - q) % n_quad * span, 1)
            packed = jnp.where(block == tile, turned, packed)
        own_gram[q] = packed
    swap = send(own_gram, mate_gram, mate)
    for k in range(chips):
        mate_copy(k).wait_send()
    for k in range(chips - 2):
        chip_copy(k).wait_send()
    for copy in direct_copies():
        copy.wait_send()
    swap.wait()
    pair_gram[...] = own_gram[...] + mate_gram[...]
    copies = [
        send(pair_gram.at[peer[1]], gram_in.at[i], peer)
        for i, peer in reversed(list(enumerate(peers))) if i
    ]
    gram_in[0] = pair_gram[quad]
    for copy in copies:
        copy.wait()
    total = jnp.zeros((8, LANES), jnp.float32)
    for i in range(chips):
        for k in range(n_quad):
            at = ((chip - i) & (chips - 1)) * n_quad + ((quad - k) & (n_quad - 1))
            total = total + gram_in[at]
    gram[...] = total


def finish_kernel(sketch_in, gram_in, sketch, gram):
    owned, cols, width = gram.shape
    sketch[...] = sketch_in[...]
    turned = gram_in[...].T
    for tile in range(-(-width // 8)):
        columns = min(8, width - tile * 8)
        for g in range(owned):
            at = (tile * owned + g) * cols
            gram[g, :, tile * 8 : tile * 8 + columns] = turned[at : at + cols, :columns]


def shards(n_wide, n_quad, basis, target, sign_bits, samples, owners):
    cols, rows = basis.shape
    devices = n_wide * n_quad
    total_samples = samples.shape[0]
    per_dev = total_samples // devices
    lines = per_dev // LANES
    scale = 1.0 / math.sqrt(rows * devices)
    chunk = rows // HIGH
    mids = chunk // LINE
    vmem = pl.BlockSpec(memory_space=pltpu.VMEM)
    f32 = jnp.float32
    half, chips = devices // 2, n_wide // 2
    flat = (8, LANES)
    packed = (lines * (cols + 1), LANES)
    kept = LANES // (cols + 1)
    blocks = mids + -(-mids // kept)
    spaces = [
        (devices, *packed), (half, *packed), (half, *packed), (chips - 2, n_quad, *packed),
        (n_quad, *packed), (n_quad, *packed), (n_quad - 1, *packed),
        (n_quad, *flat), (n_quad, *flat), (n_quad, *flat), (half, *flat),
    ]
    copies = [chips, chips - 2, n_quad, n_quad + half - 1]
    sketch, gram = pl.pallas_call(
        functools.partial(sketch_kernel, n_wide, n_quad, scale),
        out_shape=(
            jax.ShapeDtypeStruct((cols + 1, per_dev), f32),
            jax.ShapeDtypeStruct(flat, f32),
        ),
        in_specs=[
            pl.BlockSpec(memory_space=pl.ANY),
            pl.BlockSpec(memory_space=pl.ANY),
            pl.BlockSpec(memory_space=pl.ANY),
            pl.BlockSpec(memory_space=pl.ANY),
            pl.BlockSpec(memory_space=pl.ANY),
        ],
        out_specs=(vmem, vmem),
        scratch_shapes=[
            pltpu.VMEM((rows // LANES, LANES), jnp.int32),
            pltpu.VMEM((HIGH, cols, chunk), f32),
            pltpu.VMEM((rows // LANES + 2 * 8, LANES), f32),
            pltpu.SemaphoreType.DMA((3, HIGH)),
            pltpu.VMEM((chunk // LANES, LANES), f32),
            pltpu.VMEM((mids, HIGH * cols, LINE), f32),
            pltpu.VMEM((mids, cols, LINE), f32),
            pltpu.VMEM((blocks * LINE, LANES), f32),
            pltpu.VMEM((LINE, 2 * LINE), jnp.bfloat16),
            pltpu.VMEM((LANES, 2 * LANES), jnp.bfloat16),
            pltpu.VMEM((devices * lines, LANES), jnp.int32),
            pltpu.VMEM((devices * lines, LANES), jnp.int32),
            pltpu.VMEM((devices * lines, LANES), jnp.int32),
            pltpu.VMEM((devices * lines, LANES), jnp.int32),
            pltpu.VMEM((devices * lines, LANES), f32),
            pltpu.SMEM((2 * n_quad + 1, lines, LANES), jnp.int32),
            pltpu.VMEM((n_quad, per_dev, LANES), f32),
            pltpu.SemaphoreType.DMA((2,)),
            pltpu.SemaphoreType.DMA((2 * n_quad + 1,)),
        ]
        + [pltpu.VMEM(space, f32) for space in spaces]
        + [pltpu.SemaphoreType.DMA((n,)) for n in copies for _ in range(2)],
        compiler_params=pltpu.CompilerParams(
            vmem_limit_bytes=56510000, collective_id=0, has_side_effects=True
        ),
    )(
        samples.reshape(-1, LANES),
        owners.reshape(-1, LANES),
        sign_bits.reshape(-1, LANES),
        basis,
        target.reshape(-1, LANES),
    )
    sketch, gram = pl.pallas_call(
        finish_kernel,
        out_shape=(
            jax.ShapeDtypeStruct((cols + 1, per_dev), f32),
            jax.ShapeDtypeStruct((GROUPS // n_quad, cols, cols + 1), f32),
        ),
        in_specs=[vmem, vmem],
        out_specs=(vmem, vmem),
        compiler_params=pltpu.CompilerParams(vmem_limit_bytes=1024 * 1024),
    )(sketch, gram)
    return sketch.T, gram


def solution(mesh):
    placed = (P(None, ("wide", "quad")), P(("wide", "quad")), P(("wide", "quad")), P(), P())
    return jax.shard_map(
        functools.partial(shards, mesh.shape["wide"], mesh.shape["quad"]),
        mesh=mesh,
        in_specs=placed,
        out_specs=(P(("wide", "quad"), None), P("quad", None, None)),
        check_vma=False,
    )
```

```python
import functools
import math

import jax
import jax.numpy as jnp
from jax import lax
from jax.experimental import pallas as pl
from jax.experimental.pallas import tpu as pltpu
from jax.sharding import PartitionSpec as P

GROUPS = 8
LANES = 128
LINE = 256
HIGH = 8
MESH = pl.DeviceIdType.MESH


def bits_of(n):
    return n.bit_length() - 1


def parity(x, nbits):
    shift = 1
    while shift < nbits:
        x = x ^ (x >> shift)
        shift *= 2
    return x & 1


def butterfly(parts):
    half = 1
    while half < len(parts):
        for at in range(0, len(parts), 2 * half):
            for i in range(at, at + half):
                parts[i], parts[i + half] = parts[i] + parts[i + half], parts[i] - parts[i + half]
        half *= 2
    return parts


def split(x):
    top = x.astype(jnp.bfloat16)
    return top, (x - top.astype(jnp.float32)).astype(jnp.bfloat16)


def contract_last(a, b, **kw):
    return lax.dot_general(a, b, (((1,), (1,)), ((), ())), preferred_element_type=jnp.float32, **kw)


def sketch_kernel(
    n_wide, n_quad, scale, samp_in, owners_in, bits_in, x_in, t_in, sketch, gram,
    bits_all, x_all, t_all, load_sems, flips,
    field, spare, table, walsh, unit, samp, owners, picks, slot_of, sign_of, slots, rows_of, sems, pick_sems,
    mine, got, sums, wide_in, direct_in, row, quad_in, own_gram, mate_gram, pair_gram, gram_in,
    mate_sends, mate_recvs, chip_sends, chip_recvs, direct_sends, direct_recvs, sends, recvs
):
    chunk = x_all.shape[2]
    lines_in = chunk // LANES
    parts = LINE // LANES
    mids = chunk // LINE
    local_bits = bits_of(HIGH * chunk)
    cols = x_all.shape[1]
    devices = n_wide * n_quad
    lines = samp.shape[0] // devices
    per_dev = lines * LANES
    kept = LANES // (cols + 1)
    ends_at = kept * cols
    spill_blocks = -(-mids // kept)
    wide = lax.axis_index("wide")
    quad = lax.axis_index("quad")
    me = wide * n_quad + quad
    core, chip, chips = wide % 2, wide // 2, n_wide // 2
    mate = (wide + 1 - 2 * core, quad)
    peers = [
        ((chip ^ i) * 2 + core, quad ^ k)
        for i in range(chips) for k in range(n_quad)
    ]
    quad_peers = [(wide, quad ^ k) for k in range(n_quad - 1, 0, -1)]
    barrier = pltpu.get_barrier_semaphore()

    def loads(h):
        at = pl.multiple_of(h * chunk, chunk)
        rows = pl.ds(pl.multiple_of(h * lines_in, lines_in), lines_in)
        return (
            pltpu.make_async_copy(bits_in.at[rows], bits_all.at[rows], load_sems.at[0, h]),
            pltpu.make_async_copy(t_in.at[rows], t_all.at[rows], load_sems.at[1, h]),
            pltpu.make_async_copy(x_in.at[:, pl.ds(at, chunk)], x_all.at[h], load_sems.at[2, h]),
        )

    samp_copy = pltpu.make_async_copy(samp_in, samp, sems.at[0])
    owners_copy = pltpu.make_async_copy(owners_in, owners, sems.at[1])
    samp_copy.start()
    for h in range(HIGH):
        for copy in loads(h):
            copy.start()
    owners_copy.start()
    for peer in peers[1:] + [mate]:
        pl.semaphore_signal(barrier, inc=1, device_id=peer, device_id_type=MESH)
    a = lax.broadcasted_iota(jnp.int32, (LINE, LINE), 0)
    b = lax.broadcasted_iota(jnp.int32, (LINE, LINE), 1)
    line = (1 - 2 * parity(a & b, bits_of(LINE))).astype(jnp.float32).astype(jnp.bfloat16)
    walsh[:, :LINE] = line
    walsh[:, LINE:] = line
    a = lax.broadcasted_iota(jnp.int32, (LANES, LANES), 0)
    b = lax.broadcasted_iota(jnp.int32, (LANES, LANES), 1)
    line = jnp.where(a == b, 1.0, 0.0).astype(jnp.bfloat16)
    unit[:, :LANES] = line
    unit[:, LANES:] = line
    pad = t_all.shape[0] - HIGH * lines_in
    t_all[HIGH * lines_in :, :] = jnp.zeros((pad, LANES), jnp.float32)

    samp_copy.wait()
    number = samp[...]
    mid_of = (number >> bits_of(LINE)) & (mids - 1)
    high_of = (number >> bits_of(chunk)) & (HIGH - 1)
    block = jnp.zeros_like(mid_of)
    for i in range(1, spill_blocks):
        block = block + jnp.where(mid_of >= i * kept, 1, 0)
    spilled = high_of >= kept
    picks[...] = jnp.where(spilled, mids + block, mid_of) * LINE + (number & (LINE - 1))
    slot_of[...] = jnp.where(spilled, mid_of - kept * block, high_of)
    sign = parity((number >> local_bits) & me, bits_of(devices))
    sign_of[...] = (1 - 2 * sign).astype(jnp.float32) * scale

    def chip_at(k):
        return (chip + 1 + k) & (chips - 1)

    def base_of(group, own):
        to_core = (core + 1 + own) & 1
        return (chip_at(group) * 2 + to_core) * n_quad

    def even_of(turn):
        turn = jnp.minimum(turn, chips - 1)
        return jnp.maximum(turn - 1, 0), jnp.minimum(turn, 1)

    def odd_of(turn):
        own = turn >= chips - 1
        return jnp.where(own, turn, turn + 1), jnp.where(own, 1, 0)

    def even_base(turn):
        return base_of(*even_of(turn))

    def odd_base(turn):
        return base_of(*odd_of(turn))

    def fetch(dev, buf):
        at = pl.ds(dev * lines, lines)
        return pltpu.make_async_copy(picks.at[at], slots.at[buf], pick_sems.at[buf])

    def fetch_even(turn):
        base, after = even_base(turn), odd_base(turn)
        return [fetch(base + j if j < n_quad else after, j - 1) for j in range(1, n_quad + 1)]

    def fetch_odd(turn):
        base, after = odd_base(turn), even_base(turn + 1)
        return [fetch(base + j if j < n_quad else after, n_quad + j - 1) for j in range(1, n_quad + 1)]

    first_fetch = fetch(even_base(0), 2 * n_quad)
    for copy in [first_fetch] + fetch_even(0) + fetch_odd(0):
        copy.start()

    low = lax.broadcasted_iota(jnp.int32, (8, LANES), 0)
    signs = [1.0 - 2.0 * ((low >> i) & 1).astype(jnp.float32) for i in range(3)]

    def across(x, i):
        step = 1 << i
        down = pltpu.roll(x, step, 0)
        if step == 4:
            return x * signs[i] + down
        return x * signs[i] + jnp.where(signs[i] < 0, down, pltpu.roll(x, 8 - step, 0))

    def first_pass(high, carry):
        for copy in loads(high):
            copy.wait()
        rows = pl.ds(pl.multiple_of(high * lines_in, lines_in), lines_in)
        flip = (1 - 2 * bits_all[rows]).astype(jnp.float32)
        flips[...] = flip
        t = t_all[rows] * flip
        t = butterfly([t[i * 8 : i * 8 + 8] for i in range(lines_in // 8)])
        for i in range(bits_of(parts), 3):
            t = [across(x, i) for x in t]
        for i, value in enumerate(t):
            t_all[pl.ds(pl.multiple_of(high * lines_in + i * 8, 8), 8), :] = value
        x = x_all.at[high]
        at = pl.multiple_of(high * cols, cols)
        for part in range(parts):
            for tile in range(cols // 8):
                values = []
                for mid in range(mids):
                    line = mid * parts + part
                    flip = flips[pl.ds(line, 8, stride=0), :]
                    values.append(x[tile * 8 : tile * 8 + 8, line * LANES : (line + 1) * LANES] * flip)
                for mid, value in enumerate(butterfly(values)):
                    field[mid, pl.ds(at + tile * 8, 8), part * LANES : (part + 1) * LANES] = value
        return carry

    lax.fori_loop(0, HIGH, first_pass, 0)
    for i in range(lines_in // 8):
        t = butterfly([t_all[h * lines_in + i * 8 : h * lines_in + i * 8 + 8, :] for h in range(HIGH)])
        for h, value in enumerate(t):
            t_all[h * lines_in + i * 8 : h * lines_in + i * 8 + 8, :] = value
    blank = jnp.zeros((LANES - ends_at - 8, LANES), jnp.float32)

    def change(blocks, at):
        both = jnp.concatenate(split(jnp.concatenate(blocks, axis=0)), axis=1)
        out = contract_last(walsh[...], both)
        for i in range(len(blocks)):
            table[pl.ds(at + i * LINE, LINE), :] = out[:, i * LANES : (i + 1) * LANES]

    def mix(pair, carry):
        blocks = []
        for i in range(2):
            mid = 2 * pair + i
            halves = []
            for part in range(parts):
                across_lanes = slice(part * LANES, (part + 1) * LANES)
                values = [
                    butterfly([field[mid, h * cols + r : h * cols + r + 8, across_lanes] for h in range(HIGH)])
                    for r in range(0, cols, 8)
                ]
                for r, value in enumerate(values):
                    spare[mid, r * 8 : r * 8 + 8, across_lanes] = value[kept]
                t = t_all[pl.ds(mid * parts + part, 8, stride=lines_in), :]
                mains = [value[h] for h in range(kept) for value in values]
                halves.append(jnp.concatenate(mains + [t, blank], axis=0))
            blocks.append(jnp.concatenate(halves, axis=1))
        change(blocks, pl.multiple_of(pair * 2 * LINE, 2 * LINE))
        return carry

    lax.fori_loop(0, mids // 2, mix, 0, unroll=16)
    for first in range(0, spill_blocks, 2):
        blocks = []
        for i in range(first, min(first + 2, spill_blocks)):
            halves = []
            for part in range(parts):
                across_lanes = slice(part * LANES, (part + 1) * LANES)
                mains = [
                    spare[mid, :, across_lanes] if mid < mids else jnp.zeros((cols, LANES), jnp.float32)
                    for mid in range(i * kept, (i + 1) * kept)
                ]
                t = t_all[pl.ds(kept * lines_in + i * kept * parts + part, 8, stride=parts), :]
                halves.append(jnp.concatenate(mains + [t, blank], axis=0))
            blocks.append(jnp.concatenate(halves, axis=1))
        change(blocks, (mids + first) * LINE)

    def gather(buf, at):
        for r in range(per_dev):
            rows_of[at, r : r + 1, :] = table[pl.ds(slots[buf, r // LANES, r % LANES], 1), :]

    def finish(slot, dev, at):
        out = contract_last(unit[...], jnp.concatenate(split(rows_of[at]), axis=1))
        for i in range(lines):
            group = slot_of[pl.ds(dev * lines + i, 8, stride=0), :]
            sign = sign_of[pl.ds(dev * lines + i, 8, stride=0), :]
            half = out[:, i * LANES : (i + 1) * LANES]
            for r in range(0, cols, 8):
                total = half[r : r + 8]
                for g in range(1, kept):
                    total = jnp.where(group == g, half[g * cols + r : g * cols + r + 8], total)
                mine[slot, i * cols + r : i * cols + r + 8, :] = total * sign
            end = jnp.where(low == group, half[ends_at : ends_at + 8], 0.0)
            end = jnp.sum(end, axis=0, keepdims=True) * sign[:1]
            mine[slot, lines * cols + i : lines * cols + i + 1, :] = end

    def remote(src, dst, send_sem, recv_sem, peer):
        return pltpu.make_async_remote_copy(
            src_ref=src, dst_ref=dst, send_sem=send_sem, recv_sem=recv_sem,
            device_id=peer, device_id_type=MESH,
        )

    def group_of(k):
        return pl.ds(k * n_quad, n_quad)

    def mate_copy(k):
        at = group_of(k)
        return remote(mine.at[at], got.at[at], mate_sends.at[k], mate_recvs.at[k], mate)

    def chip_copy(k):
        peer = (chip_at(k) * 2 + core, quad)
        return remote(sums.at[group_of(k)], wide_in.at[k], chip_sends.at[k], chip_recvs.at[k], peer)

    def direct_copies():
        far = chips - 2
        return [
            remote(
                sums.at[far * n_quad + (quad ^ k)], direct_in.at[k], direct_sends.at[k], direct_recvs.at[k],
                (chip_at(far) * 2 + core, quad ^ k),
            )
            for k in range(n_quad - 1, -1, -1)
        ]

    def direct_arrivals():
        return [
            remote(sums.at[0], direct_in.at[k], direct_sends.at[k], direct_recvs.at[k], peers[n_quad])
            for k in range(n_quad)
        ]

    def own_sum(group):
        mate_copy(group).wait_recv()
        at = group_of(group)
        sums[at] = mine[group_of(chips + group)] + got[at]

    first_fetch.wait()
    gather(2 * n_quad, 0)
    owners_copy.wait()

    def work(step, base, buf, count):
        group, own = step
        slot = (own * chips + group) * n_quad
        for j in range(n_quad):
            if j < count:
                gather(buf + j, (j + 1) % n_quad)
            finish(slot + j, base + j, j)

    def turns(turn, carry):
        for copy in fetch_even(turn):
            copy.wait()
        work(even_of(turn), even_base(turn), 0, n_quad)

        @pl.when(turn == 0)
        def _():
            pl.semaphore_wait(barrier, len(peers))
            mate_copy(0).start()

        @pl.when((turn > 0) & (turn < chips - 1))
        def _():
            own_sum(turn - 1)
            chip_copy(turn - 1).start()

        @pl.when(turn == chips - 1)
        def _():
            own_sum(chips - 2)
            for copy in direct_copies():
                copy.start()

        @pl.when(turn < chips - 1)
        def _():
            for copy in fetch_even(turn + 1):
                copy.start()

        for copy in fetch_odd(turn):
            copy.wait()

        @pl.when(turn < chips - 1)
        def _():
            work(odd_of(turn), odd_base(turn), n_quad, n_quad)

            mate_copy(turn + 1).start()
            for copy in fetch_odd(turn + 1):
                copy.start()

        @pl.when(turn == chips - 1)
        def _():
            work(odd_of(turn), odd_base(turn), n_quad, n_quad - 1)
            own_sum(chips - 1)

        return carry

    lax.fori_loop(0, chips, turns, 0)
    for k in range(chips - 2):
        chip_copy(k).wait_recv()

    def add_row(to):
        total = sums[(chips - 1) * n_quad + to]
        for k in range(chips - 2):
            total = total + wide_in[k, to]
        row[to] = total

    sem_at = [0]

    def send(src, dst, peer):
        sem = sem_at[0]
        sem_at[0] += 1
        copy = remote(src, dst, sends.at[sem], recvs.at[sem], peer)
        copy.start()
        return copy

    copies = []
    for k, peer in enumerate(quad_peers):
        add_row(peer[1])
        copies.append(send(row.at[peer[1]], quad_in.at[k], peer))
    add_row(quad)
    for copy in copies:
        copy.wait_recv()
    sent = copies
    for copy in direct_arrivals():
        copy.wait_recv()
    total = row[quad]
    for k in range(n_quad - 1):
        total = total + quad_in[k]
    for k in range(n_quad):
        total = total + direct_in[k]
    end = jnp.concatenate([total[lines * cols + i : lines * cols + i + 1] for i in range(lines)], axis=1)
    total = jnp.concatenate([total[i * cols : (i + 1) * cols] for i in range(lines)], axis=1)
    sketch[:cols, :] = total
    sketch[cols : cols + 1, :] = end

    group = jnp.concatenate([owners[pl.ds(me * lines + i, cols, stride=0), :] for i in range(lines)], axis=1)
    first = lax.broadcasted_iota(jnp.int32, (8, per_dev), 0) == 0
    right = jnp.concatenate([total, jnp.where(first, end, 0.0)], axis=0)
    left = jnp.concatenate([jnp.where(group == g, total, 0.0) for g in range(GROUPS)], axis=0)
    part = contract_last(right, left, precision=lax.Precision.HIGHEST)
    part = part * (GROUPS / (per_dev * devices))
    span = GROUPS * cols // n_quad
    block = lax.broadcasted_iota(jnp.int32, (8, LANES), 1) // span
    for q in range(n_quad):
        packed = jnp.zeros((8, LANES), jnp.float32)
        for tile in range(part.shape[0] // 8):
            turned = part[tile * 8 : tile * 8 + 8, :]
            if (tile - q) % n_quad:
                turned = pltpu.roll(turned, (tile - q) % n_quad * span, 1)
            packed = jnp.where(block == tile, turned, packed)
        own_gram[q] = packed
    swap = send(own_gram, mate_gram, mate)
    swap.wait_recv()
    sent.append(swap)
    pair_gram[...] = own_gram[...] + mate_gram[...]
    copies = [
        send(pair_gram.at[peer[1]], gram_in.at[i], peer)
        for i, peer in reversed(list(enumerate(peers))) if i
    ]
    gram_in[0] = pair_gram[quad]
    for copy in copies:
        copy.wait_recv()
    total = jnp.zeros((8, LANES), jnp.float32)
    for i in range(chips):
        for k in range(n_quad):
            at = (chip ^ i) * n_quad + (quad ^ k)
            total = total + gram_in[at]
    gram[...] = total
    for k in range(chips):
        mate_copy(k).wait_send()
    for k in range(chips - 2):
        chip_copy(k).wait_send()
    for copy in direct_copies():
        copy.wait_send()
    for copy in sent + copies:
        copy.wait_send()


def finish_kernel(sketch_in, gram_in, sketch, gram):
    owned, cols, width = gram.shape
    sketch[...] = sketch_in[...]
    turned = gram_in[...].T
    for tile in range(-(-width // 8)):
        columns = min(8, width - tile * 8)
        for g in range(owned):
            at = (tile * owned + g) * cols
            gram[g, :, tile * 8 : tile * 8 + columns] = turned[at : at + cols, :columns]


def shards(n_wide, n_quad, basis, target, sign_bits, samples, owners):
    cols, rows = basis.shape
    devices = n_wide * n_quad
    total_samples = samples.shape[0]
    per_dev = total_samples // devices
    lines = per_dev // LANES
    scale = 1.0 / math.sqrt(rows * devices)
    chunk = rows // HIGH
    mids = chunk // LINE
    vmem = pl.BlockSpec(memory_space=pltpu.VMEM)
    f32 = jnp.float32
    half, chips = devices // 2, n_wide // 2
    flat = (8, LANES)
    packed = (lines * (cols + 1), LANES)
    kept = LANES // (cols + 1)
    blocks = mids + -(-mids // kept)
    spaces = [
        (devices, *packed), (half, *packed), (half, *packed), (chips - 2, n_quad, *packed),
        (n_quad, *packed), (n_quad, *packed), (n_quad - 1, *packed),
        (n_quad, *flat), (n_quad, *flat), (n_quad, *flat), (half, *flat),
    ]
    copies = [chips, chips - 2, n_quad, n_quad + half - 1]
    sketch, gram = pl.pallas_call(
        functools.partial(sketch_kernel, n_wide, n_quad, scale),
        out_shape=(
            jax.ShapeDtypeStruct((cols + 1, per_dev), f32),
            jax.ShapeDtypeStruct(flat, f32),
        ),
        in_specs=[
            pl.BlockSpec(memory_space=pl.ANY),
            pl.BlockSpec(memory_space=pl.ANY),
            pl.BlockSpec(memory_space=pl.ANY),
            pl.BlockSpec(memory_space=pl.ANY),
            pl.BlockSpec(memory_space=pl.ANY),
        ],
        out_specs=(vmem, vmem),
        scratch_shapes=[
            pltpu.VMEM((rows // LANES, LANES), jnp.int32),
            pltpu.VMEM((HIGH, cols, chunk), f32),
            pltpu.VMEM((rows // LANES + 2 * 8, LANES), f32),
            pltpu.SemaphoreType.DMA((3, HIGH)),
            pltpu.VMEM((chunk // LANES, LANES), f32),
            pltpu.VMEM((mids, HIGH * cols, LINE), f32),
            pltpu.VMEM((mids, cols, LINE), f32),
            pltpu.VMEM((blocks * LINE, LANES), f32),
            pltpu.VMEM((LINE, 2 * LINE), jnp.bfloat16),
            pltpu.VMEM((LANES, 2 * LANES), jnp.bfloat16),
            pltpu.VMEM((devices * lines, LANES), jnp.int32),
            pltpu.VMEM((devices * lines, LANES), jnp.int32),
            pltpu.VMEM((devices * lines, LANES), jnp.int32),
            pltpu.VMEM((devices * lines, LANES), jnp.int32),
            pltpu.VMEM((devices * lines, LANES), f32),
            pltpu.SMEM((2 * n_quad + 1, lines, LANES), jnp.int32),
            pltpu.VMEM((n_quad, per_dev, LANES), f32),
            pltpu.SemaphoreType.DMA((2,)),
            pltpu.SemaphoreType.DMA((2 * n_quad + 1,)),
        ]
        + [pltpu.VMEM(space, f32) for space in spaces]
        + [pltpu.SemaphoreType.DMA((n,)) for n in copies for _ in range(2)],
        compiler_params=pltpu.CompilerParams(
            vmem_limit_bytes=56510000, collective_id=0, has_side_effects=True
        ),
    )(
        samples.reshape(-1, LANES),
        owners.reshape(-1, LANES),
        sign_bits.reshape(-1, LANES),
        basis,
        target.reshape(-1, LANES),
    )
    sketch, gram = pl.pallas_call(
        finish_kernel,
        out_shape=(
            jax.ShapeDtypeStruct((cols + 1, per_dev), f32),
            jax.ShapeDtypeStruct((GROUPS // n_quad, cols, cols + 1), f32),
        ),
        in_specs=[vmem, vmem],
        out_specs=(vmem, vmem),
        compiler_params=pltpu.CompilerParams(vmem_limit_bytes=1024 * 1024),
    )(sketch, gram)
    return sketch.T, gram


def solution(mesh):
    placed = (P(None, ("wide", "quad")), P(("wide", "quad")), P(("wide", "quad")), P(), P())
    return jax.shard_map(
        functools.partial(shards, mesh.shape["wide"], mesh.shape["quad"]),
        mesh=mesh,
        in_specs=placed,
        out_specs=(P(("wide", "quad"), None), P("quad", None, None)),
        check_vma=False,
    )
```

```python
import functools
import math

import jax
import jax.numpy as jnp
from jax import lax
from jax.experimental import pallas as pl
from jax.experimental.pallas import tpu as pltpu
from jax.sharding import PartitionSpec as P

GROUPS = 8
LANES = 128
LINE = 256
HIGH = 8
MESH = pl.DeviceIdType.MESH


def bits_of(n):
    return n.bit_length() - 1


def parity(x, nbits):
    shift = 1
    while shift < nbits:
        x = x ^ (x >> shift)
        shift *= 2
    return x & 1


def butterfly(parts):
    half = 1
    while half < len(parts):
        for at in range(0, len(parts), 2 * half):
            for i in range(at, at + half):
                parts[i], parts[i + half] = parts[i] + parts[i + half], parts[i] - parts[i + half]
        half *= 2
    return parts


def split(x):
    top = x.astype(jnp.bfloat16)
    return top, (x - top.astype(jnp.float32)).astype(jnp.bfloat16)


def contract_last(a, b, **kw):
    return lax.dot_general(a, b, (((1,), (1,)), ((), ())), preferred_element_type=jnp.float32, **kw)


def sketch_kernel(
    n_wide, n_quad, scale, samp_in, owners_in, bits_in, x_in, t_in, sketch, gram,
    bits_all, x_all, t_all, load_sems, flips,
    field, spare, table, walsh, unit, samp, owners, picks, slot_of, sign_of, slots, rows_of, sems, pick_sems,
    mine, got, sums, wide_in, direct_in, row, quad_in, own_gram, mate_gram, pair_gram, gram_in,
    mate_sends, mate_recvs, chip_sends, chip_recvs, direct_sends, direct_recvs, sends, recvs
):
    chunk = x_all.shape[2]
    lines_in = chunk // LANES
    parts = LINE // LANES
    mids = chunk // LINE
    local_bits = bits_of(HIGH * chunk)
    cols = x_all.shape[1]
    devices = n_wide * n_quad
    lines = samp.shape[0] // devices
    per_dev = lines * LANES
    kept = LANES // (cols + 1)
    ends_at = kept * cols
    spill_blocks = -(-mids // kept)
    wide = lax.axis_index("wide")
    quad = lax.axis_index("quad")
    me = wide * n_quad + quad
    core, chip, chips = wide % 2, wide // 2, n_wide // 2
    mate = (wide + 1 - 2 * core, quad)
    peers = [
        ((chip ^ i) * 2 + core, quad ^ k)
        for i in range(chips) for k in range(n_quad)
    ]
    quad_peers = [(wide, quad ^ k) for k in range(n_quad - 1, 0, -1)]
    barrier = pltpu.get_barrier_semaphore()

    def loads(h):
        at = pl.multiple_of(h * chunk, chunk)
        rows = pl.ds(pl.multiple_of(h * lines_in, lines_in), lines_in)
        return (
            pltpu.make_async_copy(bits_in.at[rows], bits_all.at[rows], load_sems.at[0, h]),
            pltpu.make_async_copy(t_in.at[rows], t_all.at[rows], load_sems.at[1, h]),
            pltpu.make_async_copy(x_in.at[:, pl.ds(at, chunk)], x_all.at[h], load_sems.at[2, h]),
        )

    samp_copy = pltpu.make_async_copy(samp_in, samp, sems.at[0])
    owners_copy = pltpu.make_async_copy(owners_in, owners, sems.at[1])
    samp_copy.start()
    for h in range(HIGH):
        for copy in loads(h):
            copy.start()
    owners_copy.start()
    for peer in peers[1:] + [mate]:
        pl.semaphore_signal(barrier, inc=1, device_id=peer, device_id_type=MESH)
    a = lax.broadcasted_iota(jnp.int32, (LINE, LINE), 0)
    b = lax.broadcasted_iota(jnp.int32, (LINE, LINE), 1)
    line = (1 - 2 * parity(a & b, bits_of(LINE))).astype(jnp.float32).astype(jnp.bfloat16)
    walsh[:, :LINE] = line
    walsh[:, LINE:] = line
    a = lax.broadcasted_iota(jnp.int32, (LANES, LANES), 0)
    b = lax.broadcasted_iota(jnp.int32, (LANES, LANES), 1)
    line = jnp.where(a == b, 1.0, 0.0).astype(jnp.bfloat16)
    unit[:, :LANES] = line
    unit[:, LANES:] = line
    pad = t_all.shape[0] - HIGH * lines_in
    t_all[HIGH * lines_in :, :] = jnp.zeros((pad, LANES), jnp.float32)

    samp_copy.wait()
    number = samp[...]
    mid_of = (number >> bits_of(LINE)) & (mids - 1)
    high_of = (number >> bits_of(chunk)) & (HIGH - 1)
    block = jnp.zeros_like(mid_of)
    for i in range(1, spill_blocks):
        block = block + jnp.where(mid_of >= i * kept, 1, 0)
    spilled = high_of >= kept
    picks[...] = jnp.where(spilled, mids + block, mid_of) * LINE + (number & (LINE - 1))
    slot_of[...] = jnp.where(spilled, mid_of - kept * block, high_of)
    sign = parity((number >> local_bits) & me, bits_of(devices))
    sign_of[...] = (1 - 2 * sign).astype(jnp.float32) * scale

    def chip_at(k):
        return (chip + 1 + k) & (chips - 1)

    def base_of(group, own):
        to_core = (core + 1 + own) & 1
        return (chip_at(group) * 2 + to_core) * n_quad

    def even_of(turn):
        turn = jnp.minimum(turn, chips - 1)
        return jnp.maximum(turn - 1, 0), jnp.minimum(turn, 1)

    def odd_of(turn):
        own = turn >= chips - 1
        return jnp.where(own, turn, turn + 1), jnp.where(own, 1, 0)

    def even_base(turn):
        return base_of(*even_of(turn))

    def odd_base(turn):
        return base_of(*odd_of(turn))

    def fetch(dev, buf):
        at = pl.ds(dev * lines, lines)
        return pltpu.make_async_copy(picks.at[at], slots.at[buf], pick_sems.at[buf])

    def fetch_even(turn):
        base, after = even_base(turn), odd_base(turn)
        return [fetch(base + j if j < n_quad else after, j - 1) for j in range(1, n_quad + 1)]

    def fetch_odd(turn):
        base, after = odd_base(turn), even_base(turn + 1)
        return [fetch(base + j if j < n_quad else after, n_quad + j - 1) for j in range(1, n_quad + 1)]

    first_fetch = fetch(even_base(0), 2 * n_quad)
    for copy in [first_fetch] + fetch_even(0) + fetch_odd(0):
        copy.start()

    low = lax.broadcasted_iota(jnp.int32, (8, LANES), 0)
    signs = [1.0 - 2.0 * ((low >> i) & 1).astype(jnp.float32) for i in range(3)]

    def across(x, i):
        step = 1 << i
        down = pltpu.roll(x, step, 0)
        if step == 4:
            return x * signs[i] + down
        return x * signs[i] + jnp.where(signs[i] < 0, down, pltpu.roll(x, 8 - step, 0))

    def first_pass(high, carry):
        for copy in loads(high):
            copy.wait()
        rows = pl.ds(pl.multiple_of(high * lines_in, lines_in), lines_in)
        flip = (1 - 2 * bits_all[rows]).astype(jnp.float32)
        flips[...] = flip
        t = t_all[rows] * flip
        t = butterfly([t[i * 8 : i * 8 + 8] for i in range(lines_in // 8)])
        for i in range(bits_of(parts), 3):
            t = [across(x, i) for x in t]
        for i, value in enumerate(t):
            t_all[pl.ds(pl.multiple_of(high * lines_in + i * 8, 8), 8), :] = value
        x = x_all.at[high]
        at = pl.multiple_of(high * cols, cols)
        for part in range(parts):
            for tile in range(cols // 8):
                values = []
                for mid in range(mids):
                    line = mid * parts + part
                    flip = flips[pl.ds(line, 8, stride=0), :]
                    values.append(x[tile * 8 : tile * 8 + 8, line * LANES : (line + 1) * LANES] * flip)
                for mid, value in enumerate(butterfly(values)):
                    field[mid, pl.ds(at + tile * 8, 8), part * LANES : (part + 1) * LANES] = value
        return carry

    lax.fori_loop(0, HIGH, first_pass, 0)
    for i in range(lines_in // 8):
        t = butterfly([t_all[h * lines_in + i * 8 : h * lines_in + i * 8 + 8, :] for h in range(HIGH)])
        for h, value in enumerate(t):
            t_all[h * lines_in + i * 8 : h * lines_in + i * 8 + 8, :] = value
    blank = jnp.zeros((LANES - ends_at - 8, LANES), jnp.float32)

    def change(blocks, at):
        both = jnp.concatenate(split(jnp.concatenate(blocks, axis=0)), axis=1)
        out = contract_last(walsh[...], both)
        for i in range(len(blocks)):
            table[pl.ds(at + i * LINE, LINE), :] = out[:, i * LANES : (i + 1) * LANES]

    def mix(pair, carry):
        blocks = []
        for i in range(2):
            mid = 2 * pair + i
            halves = []
            for part in range(parts):
                across_lanes = slice(part * LANES, (part + 1) * LANES)
                values = [
                    butterfly([field[mid, h * cols + r : h * cols + r + 8, across_lanes] for h in range(HIGH)])
                    for r in range(0, cols, 8)
                ]
                for r, value in enumerate(values):
                    spare[mid, r * 8 : r * 8 + 8, across_lanes] = value[kept]
                t = t_all[pl.ds(mid * parts + part, 8, stride=lines_in), :]
                mains = [value[h] for h in range(kept) for value in values]
                halves.append(jnp.concatenate(mains + [t, blank], axis=0))
            blocks.append(jnp.concatenate(halves, axis=1))
        change(blocks, pl.multiple_of(pair * 2 * LINE, 2 * LINE))
        return carry

    lax.fori_loop(0, mids // 2, mix, 0, unroll=16)
    for first in range(0, spill_blocks, 2):
        blocks = []
        for i in range(first, min(first + 2, spill_blocks)):
            halves = []
            for part in range(parts):
                across_lanes = slice(part * LANES, (part + 1) * LANES)
                mains = [
                    spare[mid, :, across_lanes] if mid < mids else jnp.zeros((cols, LANES), jnp.float32)
                    for mid in range(i * kept, (i + 1) * kept)
                ]
                t = t_all[pl.ds(kept * lines_in + i * kept * parts + part, 8, stride=parts), :]
                halves.append(jnp.concatenate(mains + [t, blank], axis=0))
            blocks.append(jnp.concatenate(halves, axis=1))
        change(blocks, (mids + first) * LINE)

    def gather(buf, at):
        for r in range(per_dev):
            rows_of[at, r : r + 1, :] = table[pl.ds(slots[buf, r // LANES, r % LANES], 1), :]

    def finish(slot, dev, at):
        out = contract_last(unit[...], jnp.concatenate(split(rows_of[at]), axis=1))
        for i in range(lines):
            group = slot_of[pl.ds(dev * lines + i, 8, stride=0), :]
            sign = sign_of[pl.ds(dev * lines + i, 8, stride=0), :]
            half = out[:, i * LANES : (i + 1) * LANES]
            for r in range(0, cols, 8):
                total = half[r : r + 8]
                for g in range(1, kept):
                    total = jnp.where(group == g, half[g * cols + r : g * cols + r + 8], total)
                mine[slot, i * cols + r : i * cols + r + 8, :] = total * sign
            end = jnp.where(low == group, half[ends_at : ends_at + 8], 0.0)
            end = jnp.sum(end, axis=0, keepdims=True) * sign[:1]
            mine[slot, lines * cols + i : lines * cols + i + 1, :] = end

    def remote(src, dst, send_sem, recv_sem, peer):
        return pltpu.make_async_remote_copy(
            src_ref=src, dst_ref=dst, send_sem=send_sem, recv_sem=recv_sem,
            device_id=peer, device_id_type=MESH,
        )

    def group_of(k):
        return pl.ds(k * n_quad, n_quad)

    def mate_copy(k):
        at = group_of(k)
        return remote(mine.at[at], got.at[at], mate_sends.at[k], mate_recvs.at[k], mate)

    def chip_copy(k):
        peer = (chip_at(k) * 2 + core, quad)
        return remote(sums.at[group_of(k)], wide_in.at[k], chip_sends.at[k], chip_recvs.at[k], peer)

    def direct_copies():
        far = chips - 2
        return [
            remote(
                sums.at[far * n_quad + (quad ^ k)], direct_in.at[k], direct_sends.at[k], direct_recvs.at[k],
                (chip_at(far) * 2 + core, quad ^ k),
            )
            for k in range(n_quad - 1, -1, -1)
        ]

    def direct_arrivals():
        return [
            remote(sums.at[0], direct_in.at[k], direct_sends.at[k], direct_recvs.at[k], peers[n_quad])
            for k in range(n_quad)
        ]

    def own_sum(group):
        mate_copy(group).wait_recv()
        at = group_of(group)
        sums[at] = mine[group_of(chips + group)] + got[at]

    first_fetch.wait()
    gather(2 * n_quad, 0)
    owners_copy.wait()

    def work(step, base, buf, count):
        group, own = step
        slot = (own * chips + group) * n_quad
        for j in range(n_quad):
            if j < count:
                gather(buf + j, (j + 1) % n_quad)
            finish(slot + j, base + j, j)

    def turns(turn, carry):
        for copy in fetch_even(turn):
            copy.wait()
        work(even_of(turn), even_base(turn), 0, n_quad)

        @pl.when(turn == 0)
        def _():
            pl.semaphore_wait(barrier, len(peers))
            mate_copy(0).start()

        @pl.when((turn > 0) & (turn < chips - 1))
        def _():
            own_sum(turn - 1)
            chip_copy(turn - 1).start()

        @pl.when(turn == chips - 1)
        def _():
            own_sum(chips - 2)
            for copy in direct_copies():
                copy.start()

        @pl.when(turn < chips - 1)
        def _():
            for copy in fetch_even(turn + 1):
                copy.start()

        for copy in fetch_odd(turn):
            copy.wait()

        @pl.when(turn < chips - 1)
        def _():
            work(odd_of(turn), odd_base(turn), n_quad, n_quad)

            mate_copy(turn + 1).start()
            for copy in fetch_odd(turn + 1):
                copy.start()

        @pl.when(turn == chips - 1)
        def _():
            work(odd_of(turn), odd_base(turn), n_quad, n_quad - 1)
            own_sum(chips - 1)

        return carry

    lax.fori_loop(0, chips, turns, 0)
    for k in range(chips - 2):
        chip_copy(k).wait_recv()

    def add_row(to):
        total = sums[(chips - 1) * n_quad + to]
        for k in range(chips - 2):
            total = total + wide_in[k, to]
        row[to] = total

    sem_at = [0]

    def send(src, dst, peer):
        sem = sem_at[0]
        sem_at[0] += 1
        copy = remote(src, dst, sends.at[sem], recvs.at[sem], peer)
        copy.start()
        return copy

    copies = []
    for k, peer in enumerate(quad_peers):
        add_row(peer[1])
        copies.append(send(row.at[peer[1]], quad_in.at[k], peer))
    add_row(quad)
    for copy in copies:
        copy.wait_recv()
    sent = copies
    for copy in direct_arrivals():
        copy.wait_recv()
    total = row[quad]
    for k in range(n_quad - 1):
        total = total + quad_in[k]
    for k in range(n_quad):
        total = total + direct_in[k]
    end = jnp.concatenate([total[lines * cols + i : lines * cols + i + 1] for i in range(lines)], axis=1)
    total = jnp.concatenate([total[i * cols : (i + 1) * cols] for i in range(lines)], axis=1)
    sketch[:cols, :] = total
    sketch[cols : cols + 1, :] = end

    group = jnp.concatenate([owners[pl.ds(me * lines + i, cols, stride=0), :] for i in range(lines)], axis=1)
    first = lax.broadcasted_iota(jnp.int32, (8, per_dev), 0) == 0
    right = jnp.concatenate([total, jnp.where(first, end, 0.0)], axis=0)
    left = jnp.concatenate([jnp.where(group == g, total, 0.0) for g in range(GROUPS)], axis=0)
    right_top, right_low = split(right)
    left_top, left_low = split(left)
    part = contract_last(
        jnp.concatenate([right_top, right_top, right_low], axis=1),
        jnp.concatenate([left_top, left_low, left_top], axis=1),
    )
    part = part * (GROUPS / (per_dev * devices))
    span = GROUPS * cols // n_quad
    block = lax.broadcasted_iota(jnp.int32, (8, LANES), 1) // span
    for q in range(n_quad):
        packed = jnp.zeros((8, LANES), jnp.float32)
        for tile in range(part.shape[0] // 8):
            turned = part[tile * 8 : tile * 8 + 8, :]
            if (tile - q) % n_quad:
                turned = pltpu.roll(turned, (tile - q) % n_quad * span, 1)
            packed = jnp.where(block == tile, turned, packed)
        own_gram[q] = packed
    swap = send(own_gram, mate_gram, mate)
    swap.wait_recv()
    sent.append(swap)
    pair_gram[...] = own_gram[...] + mate_gram[...]
    copies = [
        send(pair_gram.at[peer[1]], gram_in.at[i], peer)
        for i, peer in reversed(list(enumerate(peers))) if i
    ]
    gram_in[0] = pair_gram[quad]
    for copy in copies:
        copy.wait_recv()
    total = jnp.zeros((8, LANES), jnp.float32)
    for i in range(chips):
        for k in range(n_quad):
            at = (chip ^ i) * n_quad + (quad ^ k)
            total = total + gram_in[at]
    gram[...] = total
    for k in range(chips):
        mate_copy(k).wait_send()
    for k in range(chips - 2):
        chip_copy(k).wait_send()
    for copy in direct_copies():
        copy.wait_send()
    for copy in sent + copies:
        copy.wait_send()


def finish_kernel(sketch_in, gram_in, sketch, gram):
    owned, cols, width = gram.shape
    sketch[...] = sketch_in[...]
    turned = gram_in[...].T
    for tile in range(-(-width // 8)):
        columns = min(8, width - tile * 8)
        for g in range(owned):
            at = (tile * owned + g) * cols
            gram[g, :, tile * 8 : tile * 8 + columns] = turned[at : at + cols, :columns]


def shards(n_wide, n_quad, basis, target, sign_bits, samples, owners):
    cols, rows = basis.shape
    devices = n_wide * n_quad
    total_samples = samples.shape[0]
    per_dev = total_samples // devices
    lines = per_dev // LANES
    scale = 1.0 / math.sqrt(rows * devices)
    chunk = rows // HIGH
    mids = chunk // LINE
    vmem = pl.BlockSpec(memory_space=pltpu.VMEM)
    f32 = jnp.float32
    half, chips = devices // 2, n_wide // 2
    flat = (8, LANES)
    packed = (lines * (cols + 1), LANES)
    kept = LANES // (cols + 1)
    blocks = mids + -(-mids // kept)
    spaces = [
        (devices, *packed), (half, *packed), (half, *packed), (chips - 2, n_quad, *packed),
        (n_quad, *packed), (n_quad, *packed), (n_quad - 1, *packed),
        (n_quad, *flat), (n_quad, *flat), (n_quad, *flat), (half, *flat),
    ]
    copies = [chips, chips - 2, n_quad, n_quad + half - 1]
    sketch, gram = pl.pallas_call(
        functools.partial(sketch_kernel, n_wide, n_quad, scale),
        out_shape=(
            jax.ShapeDtypeStruct((cols + 1, per_dev), f32),
            jax.ShapeDtypeStruct(flat, f32),
        ),
        in_specs=[
            pl.BlockSpec(memory_space=pl.ANY),
            pl.BlockSpec(memory_space=pl.ANY),
            pl.BlockSpec(memory_space=pl.ANY),
            pl.BlockSpec(memory_space=pl.ANY),
            pl.BlockSpec(memory_space=pl.ANY),
        ],
        out_specs=(vmem, vmem),
        scratch_shapes=[
            pltpu.VMEM((rows // LANES, LANES), jnp.int32),
            pltpu.VMEM((HIGH, cols, chunk), f32),
            pltpu.VMEM((rows // LANES + 2 * 8, LANES), f32),
            pltpu.SemaphoreType.DMA((3, HIGH)),
            pltpu.VMEM((chunk // LANES, LANES), f32),
            pltpu.VMEM((mids, HIGH * cols, LINE), f32),
            pltpu.VMEM((mids, cols, LINE), f32),
            pltpu.VMEM((blocks * LINE, LANES), f32),
            pltpu.VMEM((LINE, 2 * LINE), jnp.bfloat16),
            pltpu.VMEM((LANES, 2 * LANES), jnp.bfloat16),
            pltpu.VMEM((devices * lines, LANES), jnp.int32),
            pltpu.VMEM((devices * lines, LANES), jnp.int32),
            pltpu.VMEM((devices * lines, LANES), jnp.int32),
            pltpu.VMEM((devices * lines, LANES), jnp.int32),
            pltpu.VMEM((devices * lines, LANES), f32),
            pltpu.SMEM((2 * n_quad + 1, lines, LANES), jnp.int32),
            pltpu.VMEM((n_quad, per_dev, LANES), f32),
            pltpu.SemaphoreType.DMA((2,)),
            pltpu.SemaphoreType.DMA((2 * n_quad + 1,)),
        ]
        + [pltpu.VMEM(space, f32) for space in spaces]
        + [pltpu.SemaphoreType.DMA((n,)) for n in copies for _ in range(2)],
        compiler_params=pltpu.CompilerParams(
            vmem_limit_bytes=56510000, collective_id=0, has_side_effects=True
        ),
    )(
        samples.reshape(-1, LANES),
        owners.reshape(-1, LANES),
        sign_bits.reshape(-1, LANES),
        basis,
        target.reshape(-1, LANES),
    )
    sketch, gram = pl.pallas_call(
        finish_kernel,
        out_shape=(
            jax.ShapeDtypeStruct((cols + 1, per_dev), f32),
            jax.ShapeDtypeStruct((GROUPS // n_quad, cols, cols + 1), f32),
        ),
        in_specs=[vmem, vmem],
        out_specs=(vmem, vmem),
        compiler_params=pltpu.CompilerParams(vmem_limit_bytes=1024 * 1024),
    )(sketch, gram)
    return sketch.T, gram


def solution(mesh):
    placed = (P(None, ("wide", "quad")), P(("wide", "quad")), P(("wide", "quad")), P(), P())
    return jax.shard_map(
        functools.partial(shards, mesh.shape["wide"], mesh.shape["quad"]),
        mesh=mesh,
        in_specs=placed,
        out_specs=(P(("wide", "quad"), None), P("quad", None, None)),
        check_vma=False,
    )
```

```python
import functools
import math

import jax
import jax.numpy as jnp
from jax import lax
from jax.experimental import pallas as pl
from jax.experimental.pallas import tpu as pltpu
from jax.sharding import PartitionSpec as P

GROUPS = 8
LANES = 128
LINE = 256
HIGH = 8
MESH = pl.DeviceIdType.MESH


def bits_of(n):
    return n.bit_length() - 1


def parity(x, nbits):
    shift = 1
    while shift < nbits:
        x = x ^ (x >> shift)
        shift *= 2
    return x & 1


def butterfly(parts):
    half = 1
    while half < len(parts):
        for at in range(0, len(parts), 2 * half):
            for i in range(at, at + half):
                parts[i], parts[i + half] = parts[i] + parts[i + half], parts[i] - parts[i + half]
        half *= 2
    return parts


def split(x):
    top = x.astype(jnp.bfloat16)
    return top, (x - top.astype(jnp.float32)).astype(jnp.bfloat16)


def contract_last(a, b, **kw):
    return lax.dot_general(a, b, (((1,), (1,)), ((), ())), preferred_element_type=jnp.float32, **kw)


def sketch_kernel(
    n_wide, n_quad, scale, samp_in, owners_in, bits_in, x_in, t_in, sketch, gram,
    bits_all, x_all, t_all, load_sems, flips,
    field, spare, table, walsh, unit, samp, owners, picks, slot_of, sign_of, slots, rows_of, sems, pick_sems,
    mine, got, sums, wide_in, direct_in, row, quad_in, own_gram, mate_gram, pair_gram, gram_in,
    mate_sends, mate_recvs, chip_sends, chip_recvs, direct_sends, direct_recvs, sends, recvs
):
    chunk = x_all.shape[2]
    lines_in = chunk // LANES
    parts = LINE // LANES
    mids = chunk // LINE
    local_bits = bits_of(HIGH * chunk)
    cols = x_all.shape[1]
    devices = n_wide * n_quad
    lines = samp.shape[0] // devices
    per_dev = lines * LANES
    kept = LANES // (cols + 1)
    ends_at = kept * cols
    spill_blocks = -(-mids // kept)
    wide = lax.axis_index("wide")
    quad = lax.axis_index("quad")
    me = wide * n_quad + quad
    core, chip, chips = wide % 2, wide // 2, n_wide // 2
    mate = (wide + 1 - 2 * core, quad)
    peers = [
        ((chip ^ i) * 2 + core, quad ^ k)
        for i in range(chips) for k in range(n_quad)
    ]
    quad_peers = [(wide, quad ^ k) for k in range(n_quad - 1, 0, -1)]
    barrier = pltpu.get_barrier_semaphore()

    def loads(h):
        at = pl.multiple_of(h * chunk, chunk)
        rows = pl.ds(pl.multiple_of(h * lines_in, lines_in), lines_in)
        return (
            pltpu.make_async_copy(bits_in.at[rows], bits_all.at[rows], load_sems.at[0, h]),
            pltpu.make_async_copy(t_in.at[rows], t_all.at[rows], load_sems.at[1, h]),
            pltpu.make_async_copy(x_in.at[:, pl.ds(at, chunk)], x_all.at[h], load_sems.at[2, h]),
        )

    samp_copy = pltpu.make_async_copy(samp_in, samp, sems.at[0])
    owners_copy = pltpu.make_async_copy(owners_in, owners, sems.at[1])
    samp_copy.start()
    for h in range(HIGH):
        for copy in loads(h):
            copy.start()
    owners_copy.start()
    for peer in peers[1:] + [mate]:
        pl.semaphore_signal(barrier, inc=1, device_id=peer, device_id_type=MESH)
    a = lax.broadcasted_iota(jnp.int32, (LINE, LINE), 0)
    b = lax.broadcasted_iota(jnp.int32, (LINE, LINE), 1)
    line = (1 - 2 * parity(a & b, bits_of(LINE))).astype(jnp.float32).astype(jnp.bfloat16)
    walsh[:, :LINE] = line
    walsh[:, LINE:] = line
    a = lax.broadcasted_iota(jnp.int32, (LANES, LANES), 0)
    b = lax.broadcasted_iota(jnp.int32, (LANES, LANES), 1)
    line = jnp.where(a == b, 1.0, 0.0).astype(jnp.bfloat16)
    unit[:, :LANES] = line
    unit[:, LANES:] = line
    pad = t_all.shape[0] - HIGH * lines_in
    t_all[HIGH * lines_in :, :] = jnp.zeros((pad, LANES), jnp.float32)

    samp_copy.wait()
    number = samp[...]
    mid_of = (number >> bits_of(LINE)) & (mids - 1)
    high_of = (number >> bits_of(chunk)) & (HIGH - 1)
    block = jnp.zeros_like(mid_of)
    for i in range(1, spill_blocks):
        block = block + jnp.where(mid_of >= i * kept, 1, 0)
    spilled = high_of >= kept
    picks[...] = jnp.where(spilled, mids + block, mid_of) * LINE + (number & (LINE - 1))
    slot_of[...] = jnp.where(spilled, mid_of - kept * block, high_of)
    sign = parity((number >> local_bits) & me, bits_of(devices))
    sign_of[...] = (1 - 2 * sign).astype(jnp.float32) * scale

    def chip_at(k):
        return chip ^ (chips - 1 - k)

    def base_of(group, own):
        to_core = (core + 1 + own) & 1
        return (chip_at(group) * 2 + to_core) * n_quad

    def even_of(turn):
        turn = jnp.minimum(turn, chips - 1)
        return jnp.maximum(turn - 1, 0), jnp.minimum(turn, 1)

    def odd_of(turn):
        own = turn >= chips - 1
        return jnp.where(own, turn, turn + 1), jnp.where(own, 1, 0)

    def even_base(turn):
        return base_of(*even_of(turn))

    def odd_base(turn):
        return base_of(*odd_of(turn))

    def fetch(dev, buf):
        at = pl.ds(dev * lines, lines)
        return pltpu.make_async_copy(picks.at[at], slots.at[buf], pick_sems.at[buf])

    def fetch_even(turn):
        base, after = even_base(turn), odd_base(turn)
        return [fetch(base + j if j < n_quad else after, j - 1) for j in range(1, n_quad + 1)]

    def fetch_odd(turn):
        base, after = odd_base(turn), even_base(turn + 1)
        return [fetch(base + j if j < n_quad else after, n_quad + j - 1) for j in range(1, n_quad + 1)]

    first_fetch = fetch(even_base(0), 2 * n_quad)
    for copy in [first_fetch] + fetch_even(0) + fetch_odd(0):
        copy.start()

    low = lax.broadcasted_iota(jnp.int32, (8, LANES), 0)
    signs = [1.0 - 2.0 * ((low >> i) & 1).astype(jnp.float32) for i in range(3)]

    def across(x, i):
        step = 1 << i
        down = pltpu.roll(x, step, 0)
        if step == 4:
            return x * signs[i] + down
        return x * signs[i] + jnp.where(signs[i] < 0, down, pltpu.roll(x, 8 - step, 0))

    def first_pass(high, carry):
        for copy in loads(high):
            copy.wait()
        rows = pl.ds(pl.multiple_of(high * lines_in, lines_in), lines_in)
        flip = (1 - 2 * bits_all[rows]).astype(jnp.float32)
        flips[...] = flip
        t = t_all[rows] * flip
        t = butterfly([t[i * 8 : i * 8 + 8] for i in range(lines_in // 8)])
        for i in range(bits_of(parts), 3):
            t = [across(x, i) for x in t]
        for i, value in enumerate(t):
            t_all[pl.ds(pl.multiple_of(high * lines_in + i * 8, 8), 8), :] = value
        x = x_all.at[high]
        at = pl.multiple_of(high * cols, cols)
        for part in range(parts):
            for tile in range(cols // 8):
                values = []
                for mid in range(mids):
                    line = mid * parts + part
                    flip = flips[pl.ds(line, 8, stride=0), :]
                    values.append(x[tile * 8 : tile * 8 + 8, line * LANES : (line + 1) * LANES] * flip)
                for mid, value in enumerate(butterfly(values)):
                    field[mid, pl.ds(at + tile * 8, 8), part * LANES : (part + 1) * LANES] = value
        return carry

    lax.fori_loop(0, HIGH, first_pass, 0)
    for i in range(lines_in // 8):
        t = butterfly([t_all[h * lines_in + i * 8 : h * lines_in + i * 8 + 8, :] for h in range(HIGH)])
        for h, value in enumerate(t):
            t_all[h * lines_in + i * 8 : h * lines_in + i * 8 + 8, :] = value
    blank = jnp.zeros((LANES - ends_at - 8, LANES), jnp.float32)

    def change(blocks, at):
        both = jnp.concatenate(split(jnp.concatenate(blocks, axis=0)), axis=1)
        out = contract_last(walsh[...], both)
        for i in range(len(blocks)):
            table[pl.ds(at + i * LINE, LINE), :] = out[:, i * LANES : (i + 1) * LANES]

    def mix(pair, carry):
        blocks = []
        for i in range(2):
            mid = 2 * pair + i
            halves = []
            for part in range(parts):
                across_lanes = slice(part * LANES, (part + 1) * LANES)
                values = [
                    butterfly([field[mid, h * cols + r : h * cols + r + 8, across_lanes] for h in range(HIGH)])
                    for r in range(0, cols, 8)
                ]
                for r, value in enumerate(values):
                    spare[mid, r * 8 : r * 8 + 8, across_lanes] = value[kept]
                t = t_all[pl.ds(mid * parts + part, 8, stride=lines_in), :]
                mains = [value[h] for h in range(kept) for value in values]
                halves.append(jnp.concatenate(mains + [t, blank], axis=0))
            blocks.append(jnp.concatenate(halves, axis=1))
        change(blocks, pl.multiple_of(pair * 2 * LINE, 2 * LINE))
        return carry

    lax.fori_loop(0, mids // 2, mix, 0, unroll=16)
    for first in range(0, spill_blocks, 2):
        blocks = []
        for i in range(first, min(first + 2, spill_blocks)):
            halves = []
            for part in range(parts):
                across_lanes = slice(part * LANES, (part + 1) * LANES)
                mains = [
                    spare[mid, :, across_lanes] if mid < mids else jnp.zeros((cols, LANES), jnp.float32)
                    for mid in range(i * kept, (i + 1) * kept)
                ]
                t = t_all[pl.ds(kept * lines_in + i * kept * parts + part, 8, stride=parts), :]
                halves.append(jnp.concatenate(mains + [t, blank], axis=0))
            blocks.append(jnp.concatenate(halves, axis=1))
        change(blocks, (mids + first) * LINE)

    def gather(buf, at):
        for r in range(per_dev):
            rows_of[at, r : r + 1, :] = table[pl.ds(slots[buf, r // LANES, r % LANES], 1), :]

    def finish(slot, dev, at):
        out = contract_last(unit[...], jnp.concatenate(split(rows_of[at]), axis=1))
        for i in range(lines):
            group = slot_of[pl.ds(dev * lines + i, 8, stride=0), :]
            sign = sign_of[pl.ds(dev * lines + i, 8, stride=0), :]
            half = out[:, i * LANES : (i + 1) * LANES]
            for r in range(0, cols, 8):
                total = half[r : r + 8]
                for g in range(1, kept):
                    total = jnp.where(group == g, half[g * cols + r : g * cols + r + 8], total)
                mine[slot, i * cols + r : i * cols + r + 8, :] = total * sign
            end = jnp.where(low == group, half[ends_at : ends_at + 8], 0.0)
            end = jnp.sum(end, axis=0, keepdims=True) * sign[:1]
            mine[slot, lines * cols + i : lines * cols + i + 1, :] = end

    def remote(src, dst, send_sem, recv_sem, peer):
        return pltpu.make_async_remote_copy(
            src_ref=src, dst_ref=dst, send_sem=send_sem, recv_sem=recv_sem,
            device_id=peer, device_id_type=MESH,
        )

    def group_of(k):
        return pl.ds(k * n_quad, n_quad)

    def mate_copy(k):
        at = group_of(k)
        return remote(mine.at[at], got.at[at], mate_sends.at[k], mate_recvs.at[k], mate)

    def chip_copy(k):
        peer = (chip_at(k) * 2 + core, quad)
        return remote(sums.at[group_of(k)], wide_in.at[k], chip_sends.at[k], chip_recvs.at[k], peer)

    def direct_copies():
        far = chips - 2
        return [
            remote(
                sums.at[far * n_quad + (quad ^ k)], direct_in.at[k], direct_sends.at[k], direct_recvs.at[k],
                (chip_at(far) * 2 + core, quad ^ k),
            )
            for k in range(n_quad)
        ]

    def direct_arrivals():
        return [
            remote(sums.at[0], direct_in.at[k], direct_sends.at[k], direct_recvs.at[k], peers[n_quad])
            for k in range(n_quad)
        ]

    def own_sum(group):
        mate_copy(group).wait_recv()
        at = group_of(group)
        sums[at] = mine[group_of(chips + group)] + got[at]

    first_fetch.wait()
    gather(2 * n_quad, 0)
    owners_copy.wait()

    def work(step, base, buf, count):
        group, own = step
        slot = (own * chips + group) * n_quad
        for j in range(n_quad):
            if j < count:
                gather(buf + j, (j + 1) % n_quad)
            finish(slot + j, base + j, j)

    def turns(turn, carry):
        for copy in fetch_even(turn):
            copy.wait()
        work(even_of(turn), even_base(turn), 0, n_quad)

        @pl.when(turn == 0)
        def _():
            pl.semaphore_wait(barrier, len(peers))
            mate_copy(0).start()

        @pl.when((turn > 0) & (turn < chips - 1))
        def _():
            own_sum(turn - 1)
            chip_copy(turn - 1).start()

        @pl.when(turn == chips - 1)
        def _():
            own_sum(chips - 2)
            for copy in direct_copies():
                copy.start()

        @pl.when(turn < chips - 1)
        def _():
            for copy in fetch_even(turn + 1):
                copy.start()

        for copy in fetch_odd(turn):
            copy.wait()

        @pl.when(turn < chips - 1)
        def _():
            work(odd_of(turn), odd_base(turn), n_quad, n_quad)

            mate_copy(turn + 1).start()
            for copy in fetch_odd(turn + 1):
                copy.start()

        @pl.when(turn == chips - 1)
        def _():
            work(odd_of(turn), odd_base(turn), n_quad, n_quad - 1)
            own_sum(chips - 1)

        return carry

    lax.fori_loop(0, chips, turns, 0)
    for k in range(chips - 2):
        chip_copy(k).wait_recv()

    def add_row(to):
        total = sums[(chips - 1) * n_quad + to]
        for k in range(chips - 2):
            total = total + wide_in[k, to]
        row[to] = total

    sem_at = [0]

    def send(src, dst, peer):
        sem = sem_at[0]
        sem_at[0] += 1
        copy = remote(src, dst, sends.at[sem], recvs.at[sem], peer)
        copy.start()
        return copy

    copies = []
    for k, peer in enumerate(quad_peers):
        add_row(peer[1])
        copies.append(send(row.at[peer[1]], quad_in.at[k], peer))
    add_row(quad)
    for copy in copies:
        copy.wait_recv()
    sent = copies
    for copy in direct_arrivals():
        copy.wait_recv()
    total = row[quad]
    for k in range(n_quad - 1):
        total = total + quad_in[k]
    for k in range(n_quad):
        total = total + direct_in[k]
    end = jnp.concatenate([total[lines * cols + i : lines * cols + i + 1] for i in range(lines)], axis=1)
    total = jnp.concatenate([total[i * cols : (i + 1) * cols] for i in range(lines)], axis=1)
    sketch[:cols, :] = total
    sketch[cols : cols + 1, :] = end

    group = jnp.concatenate([owners[pl.ds(me * lines + i, cols, stride=0), :] for i in range(lines)], axis=1)
    first = lax.broadcasted_iota(jnp.int32, (8, per_dev), 0) == 0
    right = jnp.concatenate([total, jnp.where(first, end, 0.0)], axis=0)
    left = jnp.concatenate([jnp.where(group == g, total, 0.0) for g in range(GROUPS)], axis=0)
    right_top, right_low = split(right)
    left_top, left_low = split(left)
    part = contract_last(
        jnp.concatenate([right_top, right_top, right_low], axis=1),
        jnp.concatenate([left_top, left_low, left_top], axis=1),
    )
    part = part * (GROUPS / (per_dev * devices))
    span = GROUPS * cols // n_quad
    block = lax.broadcasted_iota(jnp.int32, (8, LANES), 1) // span
    for q in range(n_quad):
        packed = jnp.zeros((8, LANES), jnp.float32)
        for tile in range(part.shape[0] // 8):
            turned = part[tile * 8 : tile * 8 + 8, :]
            if (tile - q) % n_quad:
                turned = pltpu.roll(turned, (tile - q) % n_quad * span, 1)
            packed = jnp.where(block == tile, turned, packed)
        own_gram[q] = packed
    swap = send(own_gram, mate_gram, mate)
    swap.wait_recv()
    sent.append(swap)
    pair_gram[...] = own_gram[...] + mate_gram[...]
    copies = [
        send(pair_gram.at[peer[1]], gram_in.at[i], peer)
        for i, peer in reversed(list(enumerate(peers))) if i
    ]
    gram_in[0] = pair_gram[quad]
    for copy in copies:
        copy.wait_recv()
    total = jnp.zeros((8, LANES), jnp.float32)
    for i in range(chips):
        for k in range(n_quad):
            at = (chip ^ i) * n_quad + (quad ^ k)
            total = total + gram_in[at]
    gram[...] = total
    for k in range(chips):
        mate_copy(k).wait_send()
    for k in range(chips - 2):
        chip_copy(k).wait_send()
    for copy in direct_copies():
        copy.wait_send()
    for copy in sent + copies:
        copy.wait_send()


def finish_kernel(sketch_in, gram_in, sketch, gram):
    owned, cols, width = gram.shape
    sketch[...] = sketch_in[...]
    turned = gram_in[...].T
    for tile in range(-(-width // 8)):
        columns = min(8, width - tile * 8)
        for g in range(owned):
            at = (tile * owned + g) * cols
            gram[g, :, tile * 8 : tile * 8 + columns] = turned[at : at + cols, :columns]


def shards(n_wide, n_quad, basis, target, sign_bits, samples, owners):
    cols, rows = basis.shape
    devices = n_wide * n_quad
    total_samples = samples.shape[0]
    per_dev = total_samples // devices
    lines = per_dev // LANES
    scale = 1.0 / math.sqrt(rows * devices)
    chunk = rows // HIGH
    mids = chunk // LINE
    vmem = pl.BlockSpec(memory_space=pltpu.VMEM)
    f32 = jnp.float32
    half, chips = devices // 2, n_wide // 2
    flat = (8, LANES)
    packed = (lines * (cols + 1), LANES)
    kept = LANES // (cols + 1)
    blocks = mids + -(-mids // kept)
    spaces = [
        (devices, *packed), (half, *packed), (half, *packed), (chips - 2, n_quad, *packed),
        (n_quad, *packed), (n_quad, *packed), (n_quad - 1, *packed),
        (n_quad, *flat), (n_quad, *flat), (n_quad, *flat), (half, *flat),
    ]
    copies = [chips, chips - 2, n_quad, n_quad + half - 1]
    sketch, gram = pl.pallas_call(
        functools.partial(sketch_kernel, n_wide, n_quad, scale),
        out_shape=(
            jax.ShapeDtypeStruct((cols + 1, per_dev), f32),
            jax.ShapeDtypeStruct(flat, f32),
        ),
        in_specs=[
            pl.BlockSpec(memory_space=pl.ANY),
            pl.BlockSpec(memory_space=pl.ANY),
            pl.BlockSpec(memory_space=pl.ANY),
            pl.BlockSpec(memory_space=pl.ANY),
            pl.BlockSpec(memory_space=pl.ANY),
        ],
        out_specs=(vmem, vmem),
        scratch_shapes=[
            pltpu.VMEM((rows // LANES, LANES), jnp.int32),
            pltpu.VMEM((HIGH, cols, chunk), f32),
            pltpu.VMEM((rows // LANES + 2 * 8, LANES), f32),
            pltpu.SemaphoreType.DMA((3, HIGH)),
            pltpu.VMEM((chunk // LANES, LANES), f32),
            pltpu.VMEM((mids, HIGH * cols, LINE), f32),
            pltpu.VMEM((mids, cols, LINE), f32),
            pltpu.VMEM((blocks * LINE, LANES), f32),
            pltpu.VMEM((LINE, 2 * LINE), jnp.bfloat16),
            pltpu.VMEM((LANES, 2 * LANES), jnp.bfloat16),
            pltpu.VMEM((devices * lines, LANES), jnp.int32),
            pltpu.VMEM((devices * lines, LANES), jnp.int32),
            pltpu.VMEM((devices * lines, LANES), jnp.int32),
            pltpu.VMEM((devices * lines, LANES), jnp.int32),
            pltpu.VMEM((devices * lines, LANES), f32),
            pltpu.SMEM((2 * n_quad + 1, lines, LANES), jnp.int32),
            pltpu.VMEM((n_quad, per_dev, LANES), f32),
            pltpu.SemaphoreType.DMA((2,)),
            pltpu.SemaphoreType.DMA((2 * n_quad + 1,)),
        ]
        + [pltpu.VMEM(space, f32) for space in spaces]
        + [pltpu.SemaphoreType.DMA((n,)) for n in copies for _ in range(2)],
        compiler_params=pltpu.CompilerParams(
            vmem_limit_bytes=56510000, collective_id=0, has_side_effects=True
        ),
    )(
        samples.reshape(-1, LANES),
        owners.reshape(-1, LANES),
        sign_bits.reshape(-1, LANES),
        basis,
        target.reshape(-1, LANES),
    )
    sketch, gram = pl.pallas_call(
        finish_kernel,
        out_shape=(
            jax.ShapeDtypeStruct((cols + 1, per_dev), f32),
            jax.ShapeDtypeStruct((GROUPS // n_quad, cols, cols + 1), f32),
        ),
        in_specs=[vmem, vmem],
        out_specs=(vmem, vmem),
        compiler_params=pltpu.CompilerParams(vmem_limit_bytes=1024 * 1024),
    )(sketch, gram)
    return sketch.T, gram


def solution(mesh):
    placed = (P(None, ("wide", "quad")), P(("wide", "quad")), P(("wide", "quad")), P(), P())
    return jax.shard_map(
        functools.partial(shards, mesh.shape["wide"], mesh.shape["quad"]),
        mesh=mesh,
        in_specs=placed,
        out_specs=(P(("wide", "quad"), None), P("quad", None, None)),
        check_vma=False,
    )
```
